32 devices in a mesh: child: 2 (over x), row: 4 (over z), col: 4 (over y, core).
Axes of the slice: x: 2, y: 2, z: 4, core: 2. Of those that a mesh axis runs over, the one named last changes fastest.
Arguments:
- contrib: float32 [2, 2048, 2048], P('child', 'row', 'col'), may hold values from -0.125 to 0.125
- assembled: float32 [2, 2048, 4096], P('child', 'row', 'col'), may hold values from -0.125 to 0.125
- pattern: int32 [16, 16], P('row', 'col'), may hold values 0 or 1
- omega: float32 [4096, 256], P('col', 'row'), may hold values from -6 to 6
- row_maps: int32 [2, 2048], P('child'), may hold values from 0 to 4095, as said below
- leaf_bounds: int32 [4], P('row'), may hold values from 448 to 576
Outputs:
- bases: float32 [4096, 256], P('row', ('child', 'col'))
- coupling: float32 [4, 2, 256, 256], P('row', None, ('child', 'col'))
The draws below stay inside these ranges and needn't reach their ends.
Inputs may be any that keep to these rules, and one draw needn't show every extreme that they name: `row_maps`: for each child, entries k * 512 to (k + 1) * 512 - 1 are distinct, rising, and lie in k * 1024 to (k + 1) * 1024 - 1.
All inputs are finite; a program needn't handle non-finite values. No bound on the sum of `pattern` on one device may be relied on, other than what follows from the above.
Results may differ from the reference program's by a relative error of at most 0.0003.
Values sent between devices are 32-bit elements; how exact they have to be, the bound alone decides.
A program may use at most 64 MiB of HBM per device.

```python
import jax
import jax.numpy as jnp
from jax import lax

TR = 512
R = 256
BT = 256
PW = 1024
FC = 2048
PF = 4096
N_ROW = 4


def draw_row_maps(key, part):
    blocks = FC // TR
    keys = jax.random.split(jax.random.fold_in(key, 17), 2 * blocks)

    def select(single_key):
        return jnp.sort(jax.random.permutation(single_key, PW)[:TR].astype(jnp.int32))
    picked = jax.vmap(select)(keys).reshape(2, blocks, TR)
    offsets = (jnp.arange(blocks, dtype=jnp.int32) * PW)[None, :, None]
    return (picked + offsets).reshape(2, FC).astype(jnp.int32)


def set_ends(array, key, least, largest):
    index_at = [jax.random.randint(jax.random.fold_in(key, axis), (), 0, length) for axis, length in enumerate(array.shape)]
    longest = array.shape.index(max(array.shape))
    next_to = index_at[:longest] + [(index_at[longest] + 1) % array.shape[longest]] + index_at[longest + 1:]
    return array.at[tuple(index_at)].set(least).at[tuple(next_to)].set(largest)


def level_of(rng, shape, cuts, least, top_value):
    gain, own = 1.0, jax.random.fold_in(rng, 6)
    for position, blocks in cuts:
        heights = jnp.exp(jax.random.uniform(jax.random.fold_in(own, position), (blocks,), jnp.float32, least / len(cuts), top_value / len(cuts)))
        gain = gain * jnp.repeat(heights, shape[position] // blocks).reshape([-1 if axis == position else 1 for axis in range(len(shape))])
    return gain


def centred(own_key, extent, deviation, most, cuts=(), kind=jnp.bfloat16):
    drawn = jax.random.normal(own_key, extent, jnp.float32) * deviation
    if len(cuts) > 0:
        drawn = level_of(own_key, extent, cuts, -0.22, 0.18) * drawn
    return jnp.clip(drawn, min=-most, max=most).astype(kind)


def setup_inputs(seed: int = 0) -> dict:
    splits = jax.random.split(jax.random.key(seed), 7)
    return {
        "contrib": centred(splits[0], (2, FC, FC), FC ** -0.5, 0.125, ((0, 2), (1, 4), (2, 4)), jnp.float32),
        "assembled": centred(splits[1], (2, PF // 2, PF), (PF // 2) ** -0.5, 0.125, ((0, 2), (1, 4), (2, 4)), jnp.float32),
        "pattern": set_ends((jax.random.randint(splits[2], (PF // BT, PF // BT), 0, 2) < 1).astype(jnp.int32), jax.random.fold_in(splits[2], 1), 0, 1),
        "omega": centred(splits[3], (PF, R), 1.0, 6.0, ((0, 4), (1, 4)), jnp.float32),
        "row_maps": draw_row_maps(jax.random.fold_in(splits[6], 71), 0),
        "leaf_bounds": set_ends(jax.random.randint(splits[5], (N_ROW,), PW // 2 - PW // 16, PW // 2 + PW // 16 + 1), jax.random.fold_in(splits[5], 1), PW // 2 - PW // 16, (PW // 2 + PW // 16 + 1) - 1).astype(jnp.int32),
    }


highest = lax.Precision.HIGHEST

def leaf_factors(window, leaf_bound):
    positions = jnp.arange(window.shape[0], dtype=jnp.int32)
    first_leaf = (positions < leaf_bound)[:, None]
    head_count = leaf_bound.astype(jnp.float32)
    tail_count = (window.shape[0] - leaf_bound).astype(jnp.float32)
    head_gram = jnp.dot(jnp.where(first_leaf, window, 0.0).T, window, precision=highest) / head_count
    tail_gram = jnp.dot(jnp.where(first_leaf, 0.0, window).T, window, precision=highest) / tail_count
    return jnp.linalg.cholesky(jnp.stack([head_gram, tail_gram]))

def leaf_bases(window, first_leaf, factors):
    head_part = lax.linalg.triangular_solve(factors[0], window, left_side=False, lower=True, transpose_a=True)
    tail_part = lax.linalg.triangular_solve(factors[1], window, left_side=False, lower=True, transpose_a=True)
    return jnp.where(first_leaf, head_part, tail_part)

def reference(contrib, assembled, pattern, omega, row_maps, leaf_bounds):
    samples = jnp.zeros((PF, R), jnp.float32)

    def window_term(window_index):
        zero_start = jnp.zeros((), jnp.int32)
        row_start = (window_index * TR).astype(jnp.int32)
        row_block = lax.dynamic_slice(assembled, (zero_start, row_start, zero_start), (2, TR, PF)).reshape(PW, PF)
        tile_start = (window_index * (PW // BT)).astype(jnp.int32)
        tiles = lax.dynamic_slice_in_dim(pattern, tile_start, PW // BT, 0).astype(jnp.float32)
        masked = (row_block.reshape(PW // BT, BT, PF // BT, BT) * tiles[:, None, :, None]).reshape(PW, PF)
        return jnp.dot(masked, omega, precision=highest)
    samples = samples + lax.map(window_term, jnp.arange(N_ROW, dtype=jnp.int32)).reshape(PF, R)
    for child_index in range(2):
        picked = jnp.take(omega, row_maps[child_index], axis=0)
        product = jnp.dot(contrib[child_index], picked, precision=highest)
        samples = samples.at[row_maps[child_index]].add(product)
    windows = samples.reshape(N_ROW, PW, R)
    factors = jax.vmap(leaf_factors)(windows, leaf_bounds)
    positions = jnp.arange(PW, dtype=jnp.int32)
    first_leaf = (positions[None, :] < leaf_bounds[:, None])[:, :, None]
    bases = jax.vmap(leaf_bases)(windows, first_leaf, factors).reshape(PF, R)
    partner = jnp.arange(N_ROW, dtype=jnp.int32) ^ 1
    sibling = jnp.take(factors, partner, axis=0)
    coupling = jnp.einsum('wlab,wlac->wlbc', factors, sibling, precision=highest)
    return (bases, coupling)
```

```python
import functools

import jax
import jax.numpy as jnp
from jax import lax
from jax.experimental import pallas as pl
from jax.experimental.pallas import tpu as pltpu
from jax.sharding import PartitionSpec as P

BT = 256
NB = 64
SUB = 8
MESH = pl.DeviceIdType.MESH
highest = lax.Precision.HIGHEST
VMEM = pl.BlockSpec(memory_space=pltpu.VMEM)
SMEM = pl.BlockSpec(memory_space=pltpu.SMEM)

NN = (((1,), (0,)), ((), ()))
NT = (((1,), (1,)), ((), ()))
TN = (((0,), (0,)), ((), ()))


def mm(a, b, dims=NN):
    return lax.dot_general(a, b, dims, precision=highest, preferred_element_type=jnp.float32)


def split(a):
    high = a.astype(jnp.bfloat16)
    low = (a - high.astype(jnp.float32)).astype(jnp.bfloat16)
    return high, low


def dot16(a, b, dims=NN):
    return lax.dot_general(a, b, dims, preferred_element_type=jnp.float32)


def mm3(a, b, dims=NN):
    (ah, al), (bh, bl) = split(a), split(b)
    return dot16(ah, bh, dims) + (dot16(ah, bl, dims) + dot16(al, bh, dims))


def gather_kernel(own_ref, out_ref, send_right, send_left, recv, local_sem):
    count = lax.axis_size("row")
    me = lax.axis_index("row")
    has_left = me > 0
    has_right = me < count - 1
    barrier = pltpu.get_barrier_semaphore()

    @pl.when(has_left)
    def _():
        pl.semaphore_signal(barrier, inc=1, device_id={"row": me - 1}, device_id_type=MESH)

    @pl.when(has_right)
    def _():
        pl.semaphore_signal(barrier, inc=1, device_id={"row": me + 1}, device_id_type=MESH)

    keep = pltpu.make_async_copy(own_ref, out_ref.at[me], local_sem)
    keep.start()

    pl.semaphore_wait(barrier, jnp.minimum(me, 1) + jnp.minimum(count - 1 - me, 1))

    def hop(block, source, target, sems):
        return pltpu.make_async_remote_copy(
            src_ref=source,
            dst_ref=out_ref.at[block],
            send_sem=sems.at[block],
            recv_sem=recv.at[block],
            device_id={"row": target},
            device_id_type=MESH,
        )

    for step in range(count):
        low = me - step
        high = me + step
        from_left = low >= 0
        from_right = high < count
        source_low = own_ref if step == 0 else out_ref.at[low]
        source_high = own_ref if step == 0 else out_ref.at[high]
        if step > 0:

            @pl.when(from_left)
            def _():
                hop(low, source_low, me - 1, send_right).wait_recv()

        @pl.when(jnp.logical_and(from_left, has_right))
        def _():
            hop(low, source_low, me + 1, send_right).start()

        if step > 0:

            @pl.when(from_right)
            def _():
                hop(high, source_high, me + 1, send_left).wait_recv()

        @pl.when(jnp.logical_and(from_right, has_left))
        def _():
            hop(high, source_high, me - 1, send_left).start()

    for step in range(count):
        low = me - step
        high = me + step
        source_low = own_ref if step == 0 else out_ref.at[low]
        source_high = own_ref if step == 0 else out_ref.at[high]

        @pl.when(jnp.logical_and(low >= 0, has_right))
        def _():
            hop(low, source_low, me + 1, send_right).wait_send()

        @pl.when(jnp.logical_and(high < count, has_left))
        def _():
            hop(high, source_high, me - 1, send_left).wait_send()

    keep.wait()


def gather_rows(own):
    count = lax.axis_size("row")
    return pl.pallas_call(
        gather_kernel,
        out_shape=jax.ShapeDtypeStruct((count,) + own.shape, jnp.float32),
        in_specs=[VMEM],
        out_specs=VMEM,
        scratch_shapes=[
            pltpu.SemaphoreType.DMA((count,)),
            pltpu.SemaphoreType.DMA((count,)),
            pltpu.SemaphoreType.DMA((count,)),
            pltpu.SemaphoreType.DMA,
        ],
        compiler_params=pltpu.CompilerParams(collective_id=0, has_side_effects=True),
        name="gather_rows",
    )(own)


def sketch_kernel(pattern_ref, omega_ref, contrib_ref, assembled_ref, columns_ref, targets_ref, out_ref):
    half = lax.axis_index("child")
    tile_rows, tile_cols = contrib_ref.shape
    window_rows = omega_ref.shape[1]
    omega_high, omega_low = split(omega_ref[...])
    lanes = lax.broadcasted_iota(jnp.int32, (window_rows, tile_cols), 0)
    pick = jnp.where(lanes == columns_ref[...], 1.0, 0.0).astype(jnp.bfloat16)
    picked_high = dot16(omega_high, pick).astype(jnp.bfloat16)
    picked_low = dot16(omega_low, pick).astype(jnp.bfloat16)
    front_high, front_low = split(contrib_ref[...])
    product = dot16(picked_high, front_high, NT) + (
        dot16(picked_high, front_low, NT) + dot16(picked_low, front_high, NT)
    )
    product_high, product_low = split(product)
    rows = lax.broadcasted_iota(jnp.int32, (tile_rows, window_rows), 1)
    place = jnp.where(rows == targets_ref[...], 1.0, 0.0).astype(jnp.bfloat16)
    out_ref[...] = dot16(product_high, place) + dot16(product_low, place)
    for row in range(tile_rows // BT):
        blocks = []
        for col in range(window_rows // BT):
            tile = assembled_ref[row * BT : (row + 1) * BT, col * BT : (col + 1) * BT]
            blocks.append(tile * pattern_ref[half * (tile_rows // BT) + row, col].astype(jnp.float32))
        masked_high, masked_low = split(jnp.concatenate(blocks, axis=1))
        sparse = dot16(omega_high, masked_high, NT) + (
            dot16(omega_high, masked_low, NT) + dot16(omega_low, masked_high, NT)
        )
        where = pl.ds(pl.multiple_of(half * tile_rows + row * BT, BT), BT)
        out_ref[:, where] = out_ref[:, where] + sparse


def sketch(pattern, omega, contrib, assembled, columns, targets):
    return pl.pallas_call(
        sketch_kernel,
        out_shape=jax.ShapeDtypeStruct(omega.shape, jnp.float32),
        in_specs=[SMEM, VMEM, VMEM, VMEM, VMEM, VMEM],
        out_specs=VMEM,
        compiler_params=pltpu.CompilerParams(vmem_limit_bytes=48 << 20),
        name="sketch",
    )(pattern, omega, contrib, assembled, columns, targets)


def reduce_kernel(part_ref, out_ref, pair_buf, sum_buf, chip_buf, *sems):
    pair_send, pair_recv, chip_send, chip_recv, all_send, all_recv, last_send, last_recv = sems
    col_count = lax.axis_size("col")
    chips = part_ref.shape[0]
    col = lax.axis_index("col")
    group = lax.axis_index("child") * col_count + col
    chip = group // 2
    core = group % 2
    other = 1 - core

    def device(chip_index, core_index):
        flat = chip_index * 2 + core_index
        return {"child": flat // col_count, "col": flat % col_count}

    def copy(source, target, send, recv, index, device_id, recv_index):
        return pltpu.make_async_remote_copy(
            src_ref=source,
            dst_ref=target,
            send_sem=send.at[index],
            recv_sem=recv.at[recv_index],
            device_id=device_id,
            device_id_type=MESH,
        )

    order = [lax.rem(chip + step, chips) for step in range(chips)]
    partner = device(chip, other)
    barrier = pltpu.get_barrier_semaphore()
    pl.semaphore_signal(barrier, inc=1, device_id=partner, device_id_type=MESH)
    for step in range(1, chips):
        pl.semaphore_signal(barrier, inc=1, device_id=device(order[step], core), device_id_type=MESH)
    pl.semaphore_wait(barrier, chips)

    steps = list(range(1, chips)) + [0]
    pair = {}
    for step in steps:
        c = order[step]
        pair[step] = copy(part_ref.at[c, other], pair_buf.at[c], pair_send, pair_recv, c, partner, c)
        pair[step].start()
    sends = {}
    for step in range(1, chips):
        c = order[step]
        pair[step].wait_recv()
        sum_buf[c] = part_ref[c, core] + pair_buf[c]
        sends[step] = copy(sum_buf.at[c], chip_buf.at[chip], chip_send, chip_recv, c, device(c, core), chip)
        sends[step].start()
    pair[0].wait_recv()
    total = part_ref[chip, core] + pair_buf[chip]
    for step in range(1, chips):
        c = order[step]
        copy(sum_buf.at[c], chip_buf.at[c], chip_send, chip_recv, c, device(c, core), c).wait_recv()
        total = total + chip_buf[c]
    out_ref[chip, core] = total
    spread = {}
    for step in range(1, chips):
        c = order[step]
        spread[step] = copy(
            out_ref.at[chip, core], out_ref.at[chip, core], all_send, all_recv, c, device(c, core), chip
        )
        spread[step].start()
    last = {}
    last[0] = copy(out_ref.at[chip, core], out_ref.at[chip, core], last_send, last_recv, chip, partner, chip)
    last[0].start()
    for step in range(1, chips):
        c = order[step]
        copy(out_ref.at[c, core], out_ref.at[c, core], all_send, all_recv, c, device(c, core), c).wait_recv()
        last[step] = copy(out_ref.at[c, core], out_ref.at[c, core], last_send, last_recv, c, partner, c)
        last[step].start()
    for step in range(chips):
        c = order[step]
        copy(out_ref.at[c, other], out_ref.at[c, other], last_send, last_recv, c, partner, c).wait_recv()
    for step in range(chips):
        pair[step].wait_send()
        last[step].wait_send()
    for step in range(1, chips):
        sends[step].wait_send()
        spread[step].wait_send()


def reduce_windows(part):
    chips = lax.axis_size("col") * lax.axis_size("child") // 2
    columns, window_rows = part.shape
    width = columns // (2 * chips)
    part = part.reshape(chips, 2, width, window_rows)
    block = pltpu.VMEM((chips, width, window_rows), jnp.float32)
    out = pl.pallas_call(
        reduce_kernel,
        out_shape=jax.ShapeDtypeStruct(part.shape, jnp.float32),
        in_specs=[VMEM],
        out_specs=VMEM,
        scratch_shapes=[block, block, block] + [pltpu.SemaphoreType.DMA((chips,))] * 8,
        compiler_params=pltpu.CompilerParams(collective_id=1, has_side_effects=True),
        name="reduce_windows",
    )(part)
    return out.reshape(columns, window_rows)


def eliminate(leaves):
    groups = NB // SUB
    index = lax.broadcasted_iota(jnp.int32, (SUB, 2 * NB), 0)
    wide = (SUB, 2 * NB)
    leaves = [list(rows) for rows in leaves]
    for panel in range(groups):
        first = panel * SUB
        columns = [
            {
                q: [jnp.broadcast_to(rows[q][:, first + k : first + k + 1], wide) for k in range(SUB)]
                for q in range(panel, groups)
            }
            for rows in leaves
        ]
        for k in range(SUB):
            for rows, cols in zip(leaves, columns):
                own = cols[panel]
                scale = lax.rsqrt(jnp.broadcast_to(own[k][k : k + 1], wide))
                pivot = jnp.broadcast_to(rows[panel][k : k + 1], wide) * scale
                weight = {q: cols[q][k] * scale for q in range(panel, groups)}
                across = weight[panel]
                below = jnp.where(index > k, across, 0.0)
                rows[panel] = jnp.where(index == k, pivot, rows[panel] - below * pivot)
                for j in range(k + 1, SUB):
                    factor = jnp.broadcast_to(across[j : j + 1], wide)
                    for q in range(panel, groups):
                        cols[q][j] = cols[q][j] - (below if q == panel else weight[q]) * factor
                for q in range(panel + 1, groups):
                    rows[q] = rows[q] - weight[q] * pivot
    return leaves


def factor_kernel(bound_ref, window_ref, bases_ref, upper_ref, work):
    columns, window_rows = window_ref.shape
    width = bases_ref.shape[1]
    group = lax.axis_index("child") * lax.axis_size("col") + lax.axis_index("col")
    bound = bound_ref[0]
    top = window_rows // 2 + window_rows // 16
    low = window_rows // 2 - window_rows // 16
    eye = jnp.where(
        lax.broadcasted_iota(jnp.int32, (columns, columns), 0)
        == lax.broadcasted_iota(jnp.int32, (columns, columns), 1),
        1.0,
        0.0,
    )
    lane = lax.broadcasted_iota(jnp.int32, (columns, window_rows), 1)
    window = window_ref[...]
    head = jnp.where(lane < bound, window, 0.0)
    tail = window - head
    spans = ((head, 0, (top + 127) // 128 * 128), (tail, low // 128 * 128, window_rows))
    counts = (bound, window_rows - bound)
    for leaf, (masked, start, stop) in enumerate(spans):
        part = masked[:, start:stop]
        gram = mm3(part, part, NT)
        work[leaf, :, :columns] = gram / counts[leaf].astype(jnp.float32)
        work[leaf, :, columns:] = eye
    small_eye = eye[:NB, :NB]
    for block in range(columns // NB):
        begin, end = block * NB, (block + 1) * NB
        aug = []
        for leaf in range(2):
            diagonal = jnp.concatenate([work[leaf, begin:end, begin:end], small_eye], axis=1)
            aug.append([diagonal[q * SUB : (q + 1) * SUB] for q in range(NB // SUB)])
        done = eliminate(aug)
        for leaf in range(2):
            inverse = jnp.concatenate(done[leaf], axis=0)[:, NB:]
            rows = mm(inverse, work[leaf, begin:end, :])
            work[leaf, begin:end, :] = rows
            if end < columns:
                work[leaf, end:, :] = work[leaf, end:, :] - mm3(rows[:, end:columns], rows, TN)
    keep = lax.broadcasted_iota(jnp.int32, (columns, columns), 1) >= lax.broadcasted_iota(
        jnp.int32, (columns, columns), 0
    )
    for leaf in range(2):
        upper_ref[leaf] = jnp.where(keep, work[leaf, :, :columns], 0.0)
    mine = pl.ds(pl.multiple_of(group * width, width), width)
    inverse = jnp.concatenate([work[0, mine, columns:], work[1, mine, columns:]], axis=0)
    both = mm3(inverse, window)
    lane = lax.broadcasted_iota(jnp.int32, (width, window_rows), 1)
    bases_ref[...] = jnp.where(lane < bound, both[:width], both[width:]).T


def factor(bound, window):
    columns, window_rows = window.shape
    width = columns // (2 * lax.axis_size("col"))
    return pl.pallas_call(
        factor_kernel,
        out_shape=(
            jax.ShapeDtypeStruct((window_rows, width), jnp.float32),
            jax.ShapeDtypeStruct((2, columns, columns), jnp.float32),
        ),
        in_specs=[SMEM, VMEM],
        out_specs=(VMEM, VMEM),
        scratch_shapes=[pltpu.VMEM((2, columns, 2 * columns), jnp.float32)],
        compiler_params=pltpu.CompilerParams(vmem_limit_bytes=48 << 20),
        name="factor",
    )(bound, window)


def couple_kernel(own_ref, sibling_ref, out_ref):
    width = out_ref.shape[2]
    group = lax.axis_index("child") * lax.axis_size("col") + lax.axis_index("col")
    mine = pl.ds(pl.multiple_of(group * width, width), width)
    for leaf in range(2):
        out_ref[0, leaf] = mm3(own_ref[leaf, mine, :], sibling_ref[leaf], NT)


def couple(own, sibling):
    columns = own.shape[1]
    width = columns // (2 * lax.axis_size("col"))
    return pl.pallas_call(
        couple_kernel,
        out_shape=jax.ShapeDtypeStruct((1, 2, width, columns), jnp.float32),
        in_specs=[VMEM, VMEM],
        out_specs=VMEM,
        name="couple",
    )(own, sibling)


def sibling_of(block):
    count = lax.axis_size("row")
    return lax.ppermute(block, "row", [(k, k ^ 1) for k in range(count)])


def local(contrib, assembled, pattern, omega, row_maps, leaf_bounds):
    tile_rows, tile_cols = contrib.shape[1:]
    window_rows = omega.shape[0]
    row_pos = lax.axis_index("row")
    col_pos = lax.axis_index("col")
    child_maps = row_maps[0]
    columns = lax.dynamic_slice_in_dim(child_maps, col_pos * tile_cols, tile_cols) - col_pos * window_rows
    targets = lax.dynamic_slice_in_dim(child_maps, row_pos * tile_rows, tile_rows) - row_pos * window_rows
    gathered = gather_rows(omega.T).reshape(-1, window_rows)
    part = sketch(pattern, gathered, contrib[0], assembled[0], columns[None, :], targets[:, None])
    window = reduce_windows(part)
    bases, upper = factor(leaf_bounds, window)
    coupling = couple(upper, sibling_of(upper))
    return (bases, coupling)


def solution(mesh):
    in_specs = (
        P("child", "row", "col"),
        P("child", "row", "col"),
        P("row", "col"),
        P("col", "row"),
        P("child", None),
        P("row"),
    )
    out_specs = (P("row", ("child", "col")), P("row", None, ("child", "col"), None))
    return jax.shard_map(local, mesh=mesh, in_specs=in_specs, out_specs=out_specs, check_vma=False)
```

```python
import jax
import jax.numpy as jnp
from jax import lax
from jax.experimental import pallas as pl
from jax.experimental.pallas import tpu as pltpu
from jax.sharding import PartitionSpec as P

BT = 256
NB = 64
SUB = 8
MESH = pl.DeviceIdType.MESH
highest = lax.Precision.HIGHEST
VMEM = pl.BlockSpec(memory_space=pltpu.VMEM)
SMEM = pl.BlockSpec(memory_space=pltpu.SMEM)

NN = (((1,), (0,)), ((), ()))
NT = (((1,), (1,)), ((), ()))
TN = (((0,), (0,)), ((), ()))


def mm(a, b, dims=NN):
    return lax.dot_general(a, b, dims, precision=highest, preferred_element_type=jnp.float32)


def split(a):
    high = a.astype(jnp.bfloat16)
    low = (a - high.astype(jnp.float32)).astype(jnp.bfloat16)
    return high, low


def dot16(a, b, dims=NN):
    return lax.dot_general(a, b, dims, preferred_element_type=jnp.float32)


def mm3(a, b, dims=NN):
    (ah, al), (bh, bl) = split(a), split(b)
    return dot16(ah, bh, dims) + (dot16(ah, bl, dims) + dot16(al, bh, dims))


class Plane:
    def __init__(self):
        self.cols = lax.axis_size("col")
        self.chips = self.cols * lax.axis_size("child") // 2
        self.group = lax.axis_index("child") * self.cols + lax.axis_index("col")
        self.chip = self.group // 2
        self.core = self.group % 2
        self.order = [lax.rem(self.chip + step, self.chips) for step in range(self.chips)]

    def device(self, chip, core):
        flat = chip * 2 + core
        return {"child": flat // self.cols, "col": flat % self.cols}


def remote(source, target, send_sem, recv_sem, device):
    return pltpu.make_async_remote_copy(
        src_ref=source, dst_ref=target, send_sem=send_sem, recv_sem=recv_sem, device_id=device, device_id_type=MESH
    )


def greet(plane):
    count = lax.axis_size("row")
    me = lax.axis_index("row")
    barrier = pltpu.get_barrier_semaphore()

    @pl.when(me > 0)
    def _():
        pl.semaphore_signal(barrier, inc=1, device_id={"row": me - 1}, device_id_type=MESH)

    @pl.when(me < count - 1)
    def _():
        pl.semaphore_signal(barrier, inc=1, device_id={"row": me + 1}, device_id_type=MESH)

    pl.semaphore_signal(barrier, inc=1, device_id=plane.device(plane.chip, 1 - plane.core), device_id_type=MESH)
    for step in range(1, plane.chips):
        pl.semaphore_signal(
            barrier, inc=1, device_id=plane.device(plane.order[step], plane.core), device_id_type=MESH
        )
    pl.semaphore_wait(barrier, plane.chips + jnp.minimum(me, 1) + jnp.minimum(count - 1 - me, 1))


def gather(own_ref, out_ref, sems, prepare):
    send_right, send_left, recv, swap_send, swap_recv, local_sem = sems
    count = lax.axis_size("row")
    me = lax.axis_index("row")
    half = lax.axis_index("child")
    has_left = me > 0
    has_right = me < count - 1
    keep = pltpu.make_async_copy(own_ref, out_ref.at[me], local_sem)
    keep.start()

    def hop(block, target, step, send):
        source = own_ref.at[half] if step == 0 else out_ref.at[block, half]
        return remote(source, out_ref.at[block, half], send.at[block], recv.at[block], {"row": target})

    def swap(block):
        place = out_ref.at[block, half]
        return remote(place, place, swap_send.at[block], swap_recv.at[block], {"child": 1 - half})

    for step in range(count):
        low = me - step
        high = me + step
        if step > 0:

            @pl.when(low >= 0)
            def _():
                hop(low, me - 1, step, send_right).wait_recv()

        @pl.when(jnp.logical_and(low >= 0, has_right))
        def _():
            hop(low, me + 1, step, send_right).start()

        if step > 0:

            @pl.when(low >= 0)
            def _():
                swap(low).start()

            @pl.when(high < count)
            def _():
                hop(high, me + 1, step, send_left).wait_recv()

        @pl.when(jnp.logical_and(high < count, has_left))
        def _():
            hop(high, me - 1, step, send_left).start()

        if step > 0:

            @pl.when(high < count)
            def _():
                swap(high).start()

        if step == 0:
            prepare()

    keep.wait()
    for step in range(1, count):
        block = lax.rem(me + step, count)
        place = out_ref.at[block, 1 - half]
        remote(place, place, swap_send.at[block], swap_recv.at[block], {"child": 1 - half}).wait_recv()

    def drain():
        for step in range(count):
            low = me - step
            high = me + step

            @pl.when(jnp.logical_and(low >= 0, has_right))
            def _():
                hop(low, me + 1, step, send_right).wait_send()

            @pl.when(jnp.logical_and(high < count, has_left))
            def _():
                hop(high, me - 1, step, send_left).wait_send()

        for step in range(1, count):
            swap(lax.rem(me + step, count)).wait_send()

    return drain


def prepare_sketch(pattern_ref, contrib, assembled, columns_ref, targets_ref, held):
    pick, place, front, entries = held
    half = lax.axis_index("child")
    tile_rows, tile_cols = contrib.shape
    window_rows = assembled.shape[1]
    lanes = lax.broadcasted_iota(jnp.int32, (window_rows, tile_cols), 0)
    pick[...] = jnp.where(lanes == columns_ref[...], 1.0, 0.0).astype(jnp.bfloat16)
    rows = lax.broadcasted_iota(jnp.int32, (tile_rows, window_rows), 1)
    place[...] = jnp.where(rows == targets_ref[...], 1.0, 0.0).astype(jnp.bfloat16)
    front[0], front[1] = split(contrib[...])
    for row in range(tile_rows // BT):
        for col in range(window_rows // BT):
            where = (slice(row * BT, (row + 1) * BT), slice(col * BT, (col + 1) * BT))
            present = pattern_ref[half * (tile_rows // BT) + row, col].astype(jnp.float32)
            entries[(0,) + where], entries[(1,) + where] = split(assembled[where] * present)


def sketch(omega, held, part_ref):
    pick, place, front, entries = held
    half = lax.axis_index("child")
    tile_rows = place.shape[0]
    omega_high, omega_low = split(omega)
    picked_high = dot16(omega_high, pick[...]).astype(jnp.bfloat16)
    picked_low = dot16(omega_low, pick[...]).astype(jnp.bfloat16)
    product = dot16(picked_high, front[0], NT) + (
        dot16(picked_high, front[1], NT) + dot16(picked_low, front[0], NT)
    )
    sparse = dot16(omega_high, entries[0], NT) + (
        dot16(omega_high, entries[1], NT) + dot16(omega_low, entries[0], NT)
    )
    product_high, product_low = split(product)
    part_ref[...] = (dot16(product_high, place[...]) + dot16(product_low, place[...])).reshape(part_ref.shape)
    where = pl.ds(pl.multiple_of(half * tile_rows, tile_rows), tile_rows)
    part_ref[:, :, :, where] = part_ref[:, :, :, where] + sparse.reshape(part_ref.shape[:3] + (tile_rows,))


def reduce(plane, part_ref, out_ref, pair_buf, sum_buf, chip_buf, sems):
    pair_send, pair_recv, chip_send, chip_recv, all_send, all_recv, last_send, last_recv = sems
    chips, chip, core, order = plane.chips, plane.chip, plane.core, plane.order
    other = 1 - core
    partner = plane.device(chip, other)

    def copy(source, target, send, recv, index, device, recv_index):
        return remote(source, target, send.at[index], recv.at[recv_index], device)

    steps = list(range(1, chips)) + [0]
    pair = {}
    for step in steps:
        c = order[step]
        pair[step] = copy(part_ref.at[c, other], pair_buf.at[c], pair_send, pair_recv, c, partner, c)
        pair[step].start()
    sends = {}
    for step in range(1, chips):
        c = order[step]
        pair[step].wait_recv()
        sum_buf[c] = part_ref[c, core] + pair_buf[c]
        sends[step] = copy(sum_buf.at[c], chip_buf.at[chip], chip_send, chip_recv, c, plane.device(c, core), chip)
        sends[step].start()
    pair[0].wait_recv()
    total = part_ref[chip, core] + pair_buf[chip]
    for step in range(1, chips):
        c = order[step]
        copy(sum_buf.at[c], chip_buf.at[c], chip_send, chip_recv, c, plane.device(c, core), c).wait_recv()
        total = total + chip_buf[c]
    out_ref[chip, core] = total
    own = out_ref.at[chip, core]
    spread = {}
    for step in range(1, chips):
        c = order[step]
        spread[step] = copy(own, own, all_send, all_recv, c, plane.device(c, core), chip)
        spread[step].start()
    last = {}
    last[0] = copy(own, own, last_send, last_recv, chip, partner, chip)
    last[0].start()
    for step in range(1, chips):
        c = order[step]
        block = out_ref.at[c, core]
        copy(block, block, all_send, all_recv, c, plane.device(c, core), c).wait_recv()
        last[step] = copy(block, block, last_send, last_recv, c, partner, c)
        last[step].start()
    for step in range(chips):
        c = order[step]
        block = out_ref.at[c, other]
        copy(block, block, last_send, last_recv, c, partner, c).wait_recv()

    def drain():
        for step in range(chips):
            pair[step].wait_send()
            last[step].wait_send()
        for step in range(1, chips):
            sends[step].wait_send()
            spread[step].wait_send()

    return drain


def eliminate(leaves):
    groups = NB // SUB
    index = lax.broadcasted_iota(jnp.int32, (SUB, 2 * NB), 0)
    wide = (SUB, 2 * NB)
    leaves = [list(rows) for rows in leaves]
    for panel in range(groups):
        first = panel * SUB
        columns = [
            {
                q: [jnp.broadcast_to(rows[q][:, first + k : first + k + 1], wide) for k in range(SUB)]
                for q in range(panel, groups)
            }
            for rows in leaves
        ]
        for k in range(SUB):
            for rows, cols in zip(leaves, columns):
                own = cols[panel]
                scale = lax.rsqrt(jnp.broadcast_to(own[k][k : k + 1], wide))
                pivot = jnp.broadcast_to(rows[panel][k : k + 1], wide) * scale
                weight = {q: cols[q][k] * scale for q in range(panel, groups)}
                across = weight[panel]
                below = jnp.where(index > k, across, 0.0)
                rows[panel] = jnp.where(index == k, pivot, rows[panel] - below * pivot)
                for j in range(k + 1, SUB):
                    factor = jnp.broadcast_to(across[j : j + 1], wide)
                    for q in range(panel, groups):
                        cols[q][j] = cols[q][j] - (below if q == panel else weight[q]) * factor
                for q in range(panel + 1, groups):
                    rows[q] = rows[q] - weight[q] * pivot
    return leaves


def factor(bound, window, work, done_block):
    columns, window_rows = window.shape
    top = window_rows // 2 + window_rows // 16
    low = window_rows // 2 - window_rows // 16
    eye = jnp.where(
        lax.broadcasted_iota(jnp.int32, (columns, columns), 0)
        == lax.broadcasted_iota(jnp.int32, (columns, columns), 1),
        1.0,
        0.0,
    )
    lane = lax.broadcasted_iota(jnp.int32, (columns, window_rows), 1)
    head = jnp.where(lane < bound, window, 0.0)
    tail = window - head
    spans = ((head, 0, (top + 127) // 128 * 128), (tail, low // 128 * 128, window_rows))
    counts = (bound, window_rows - bound)
    for leaf, (masked, start, stop) in enumerate(spans):
        part = masked[:, start:stop]
        gram = mm3(part, part, NT)
        work[leaf, :, :columns] = gram / counts[leaf].astype(jnp.float32)
        work[leaf, :, columns:] = eye
    small_eye = eye[:NB, :NB]
    for block in range(columns // NB):
        begin, end = block * NB, (block + 1) * NB
        aug = []
        for leaf in range(2):
            diagonal = jnp.concatenate([work[leaf, begin:end, begin:end], small_eye], axis=1)
            aug.append([diagonal[q * SUB : (q + 1) * SUB] for q in range(NB // SUB)])
        done = eliminate(aug)
        for leaf in range(2):
            inverse = jnp.concatenate(done[leaf], axis=0)[:, NB:]
            rows = mm(inverse, work[leaf, begin:end, :])
            work[leaf, begin:end, :] = rows
            done_block(leaf, block, begin, end, rows[:, :columns])
            if end < columns:
                work[leaf, end:, :] = work[leaf, end:, :] - mm3(rows[:, end:columns], rows, TN)


def whole_kernel(
    bound_ref, pattern_ref, omega_ref, contrib_ref, assembled_ref, columns_ref, targets_ref, bases_ref, coupling_ref,
    gathered, contrib_buf, assembled_buf, pick, place, front, entries,
    part, window, pair_buf, sum_buf, chip_buf, work, upper, sibling, input_sems, *sems,
):
    plane = Plane()
    window_rows = assembled_buf.shape[1]
    columns, width = upper.shape[1], bases_ref.shape[0]
    held = (pick, place, front, entries)
    load_front = pltpu.make_async_copy(contrib_ref.at[0], contrib_buf, input_sems.at[0])
    load_entries = pltpu.make_async_copy(assembled_ref.at[0], assembled_buf, input_sems.at[1])
    load_front.start()
    load_entries.start()
    greet(plane)

    def prepare():
        load_front.wait()
        load_entries.wait()
        prepare_sketch(pattern_ref, contrib_buf, assembled_buf, columns_ref, targets_ref, held)

    drain_gather = gather(omega_ref, gathered, sems[:6], prepare)
    sketch(gathered[...].reshape(columns, window_rows), held, part)
    drain_reduce = reduce(plane, part, window, pair_buf, sum_buf, chip_buf, sems[6:14])
    drain_gather()
    drain_reduce()

    near_send, near_recv = sems[14:]
    row_pos = lax.axis_index("row")
    near = {"row": row_pos + 1 - 2 * (row_pos % 2)}

    def send(leaf, block):
        start = block * NB // 128 * 128
        rows = slice(block * NB, (block + 1) * NB)
        source, target = upper.at[leaf, rows, start:], sibling.at[leaf, rows, start:]
        return remote(source, target, near_send.at[leaf, block], near_recv.at[leaf, block], near)

    def done_block(leaf, block, begin, end, rows):
        keep = lax.broadcasted_iota(jnp.int32, rows.shape, 1) >= begin + lax.broadcasted_iota(
            jnp.int32, rows.shape, 0
        )
        upper[leaf, begin:end, :] = jnp.where(keep, rows, 0.0)
        send(leaf, block).start()

    bound = bound_ref[0]
    samples = window[...].reshape(columns, window_rows)
    factor(bound, samples, work, done_block)
    mine = pl.ds(pl.multiple_of(plane.group * width, width), width)
    inverse = jnp.concatenate([work[0, mine, columns:], work[1, mine, columns:]], axis=0)
    both = mm3(inverse, samples)
    lane = lax.broadcasted_iota(jnp.int32, (width, window_rows), 1)
    bases_ref[...] = jnp.where(lane < bound, both[:width], both[width:])
    for leaf in range(2):
        own = upper[leaf, mine, :]
        pieces = []
        for block in range(columns // NB):
            start = block * NB // 128 * 128
            send(leaf, block).wait_recv()
            pieces.append(mm3(own[:, start:], sibling[leaf, block * NB : (block + 1) * NB, start:], NT))
        coupling_ref[0, leaf] = jnp.concatenate(pieces, axis=1)
    for leaf in range(2):
        for block in range(columns // NB):
            send(leaf, block).wait_send()


def local(contrib, assembled, pattern, omega, row_maps, leaf_bounds):
    tile_rows, tile_cols = contrib.shape[1:]
    window_rows, own_width = omega.shape
    rows = lax.axis_size("row")
    chips = lax.axis_size("col") * lax.axis_size("child") // 2
    columns = own_width * rows
    width = columns // (2 * chips)
    row_pos = lax.axis_index("row")
    col_pos = lax.axis_index("col")
    child_maps = row_maps[0]
    col_maps = lax.dynamic_slice_in_dim(child_maps, col_pos * tile_cols, tile_cols) - col_pos * window_rows
    targets = lax.dynamic_slice_in_dim(child_maps, row_pos * tile_rows, tile_rows) - row_pos * window_rows
    own = omega.T.reshape(2, own_width // 2, window_rows)
    f32, bf16, dma = jnp.float32, jnp.bfloat16, pltpu.SemaphoreType.DMA
    any_space = pl.BlockSpec(memory_space=pl.ANY)
    block = pltpu.VMEM((chips, width, window_rows), f32)
    split_window = pltpu.VMEM((chips, 2, width, window_rows), f32)
    bases, coupling = pl.pallas_call(
        whole_kernel,
        out_shape=(
            jax.ShapeDtypeStruct((width, window_rows), f32),
            jax.ShapeDtypeStruct((1, 2, width, columns), f32),
        ),
        in_specs=[SMEM, SMEM, VMEM, any_space, any_space, VMEM, VMEM],
        out_specs=(VMEM, VMEM),
        scratch_shapes=[
            pltpu.VMEM((rows, 2, own_width // 2, window_rows), f32),
            pltpu.VMEM((tile_rows, tile_cols), f32),
            pltpu.VMEM((tile_rows, window_rows), f32),
            pltpu.VMEM((window_rows, tile_cols), bf16),
            pltpu.VMEM((tile_rows, window_rows), bf16),
            pltpu.VMEM((2, tile_rows, tile_cols), bf16),
            pltpu.VMEM((2, tile_rows, window_rows), bf16),
            split_window,
            split_window,
            block,
            block,
            block,
            pltpu.VMEM((2, columns, 2 * columns), f32),
            pltpu.VMEM((2, columns, columns), f32),
            pltpu.VMEM((2, columns, columns), f32),
            dma((2,)),
        ]
        + [dma((rows,))] * 5
        + [dma]
        + [dma((chips,))] * 8
        + [dma((2, columns // NB))] * 2,
        compiler_params=pltpu.CompilerParams(
            collective_id=0, has_side_effects=True, vmem_limit_bytes=56 << 20
        ),
        name="front_samples",
    )(leaf_bounds, pattern, own, contrib, assembled, col_maps[None, :], targets[:, None])
    return (bases.T, coupling)


def solution(mesh):
    in_specs = (
        P("child", "row", "col"),
        P("child", "row", "col"),
        P("row", "col"),
        P("col", "row"),
        P("child", None),
        P("row"),
    )
    out_specs = (P("row", ("child", "col")), P("row", None, ("child", "col"), None))
    return jax.shard_map(local, mesh=mesh, in_specs=in_specs, out_specs=out_specs, check_vma=False)
```

```python
import jax
import jax.numpy as jnp
from jax import lax
from jax.experimental import pallas as pl
from jax.experimental.pallas import tpu as pltpu
from jax.sharding import PartitionSpec as P

BT = 256
NB = 64
SUB = 8
MESH = pl.DeviceIdType.MESH
highest = lax.Precision.HIGHEST
VMEM = pl.BlockSpec(memory_space=pltpu.VMEM)
SMEM = pl.BlockSpec(memory_space=pltpu.SMEM)

NN = (((1,), (0,)), ((), ()))
NT = (((1,), (1,)), ((), ()))
TN = (((0,), (0,)), ((), ()))


def mm(a, b, dims=NN):
    return lax.dot_general(a, b, dims, precision=highest, preferred_element_type=jnp.float32)


def split(a):
    high = a.astype(jnp.bfloat16)
    low = (a - high.astype(jnp.float32)).astype(jnp.bfloat16)
    return high, low


def dot16(a, b, dims=NN):
    return lax.dot_general(a, b, dims, preferred_element_type=jnp.float32)


def mm3(a, b, dims=NN):
    (ah, al), (bh, bl) = split(a), split(b)
    return dot16(ah, bh, dims) + (dot16(ah, bl, dims) + dot16(al, bh, dims))


class Plane:
    def __init__(self):
        self.cols = lax.axis_size("col")
        self.chips = self.cols * lax.axis_size("child") // 2
        self.group = lax.axis_index("child") * self.cols + lax.axis_index("col")
        self.chip = self.group // 2
        self.core = self.group % 2
        self.order = [lax.rem(self.chip + step, self.chips) for step in range(self.chips)]

    def device(self, chip, core):
        flat = chip * 2 + core
        return {"child": flat // self.cols, "col": flat % self.cols}


def remote(source, target, send_sem, recv_sem, device):
    return pltpu.make_async_remote_copy(
        src_ref=source, dst_ref=target, send_sem=send_sem, recv_sem=recv_sem, device_id=device, device_id_type=MESH
    )


def greet(plane):
    count = lax.axis_size("row")
    me = lax.axis_index("row")
    barrier = pltpu.get_barrier_semaphore()

    @pl.when(me > 0)
    def _():
        pl.semaphore_signal(barrier, inc=1, device_id={"row": me - 1}, device_id_type=MESH)

    @pl.when(me < count - 1)
    def _():
        pl.semaphore_signal(barrier, inc=1, device_id={"row": me + 1}, device_id_type=MESH)

    pl.semaphore_signal(barrier, inc=1, device_id=plane.device(plane.chip, 1 - plane.core), device_id_type=MESH)
    for step in range(1, plane.chips):
        pl.semaphore_signal(
            barrier, inc=1, device_id=plane.device(plane.order[step], plane.core), device_id_type=MESH
        )
    pl.semaphore_wait(barrier, plane.chips + jnp.minimum(me, 1) + jnp.minimum(count - 1 - me, 1))


def gather(own_ref, out_ref, sems, prepare, stage, settle):
    send_right, send_left, recv, swap_send, swap_recv, local_sem = sems
    count = lax.axis_size("row")
    me = lax.axis_index("row")
    half = lax.axis_index("child")
    has_left = me > 0
    has_right = me < count - 1
    keep = pltpu.make_async_copy(own_ref, out_ref.at[me], local_sem)
    keep.start()

    def hop(block, target, step, send):
        source = own_ref.at[half] if step == 0 else out_ref.at[block, half]
        return remote(source, out_ref.at[block, half], send.at[block], recv.at[block], {"row": target})

    def swap(block):
        place = out_ref.at[block, half]
        return remote(place, place, swap_send.at[block], swap_recv.at[block], {"child": 1 - half})

    def at_distance(step, act):
        for block, there in ((me - step, me >= step), (me + step, me + step < count)):

            @pl.when(there)
            def _():
                act(block)

    def wait_swap(block):
        place = out_ref.at[block, 1 - half]
        remote(place, place, swap_send.at[block], swap_recv.at[block], {"child": 1 - half}).wait_recv()

    def staged(block):
        wait_swap(block)
        stage(block)

    for step in range(count):
        low = me - step
        high = me + step
        if step > 0:

            @pl.when(low >= 0)
            def _():
                hop(low, me - 1, step, send_right).wait_recv()

        @pl.when(jnp.logical_and(low >= 0, has_right))
        def _():
            hop(low, me + 1, step, send_right).start()

        if step > 0:

            @pl.when(low >= 0)
            def _():
                swap(low).start()

            @pl.when(high < count)
            def _():
                hop(high, me + 1, step, send_left).wait_recv()

        @pl.when(jnp.logical_and(high < count, has_left))
        def _():
            hop(high, me - 1, step, send_left).start()

        if step > 0:

            @pl.when(high < count)
            def _():
                swap(high).start()

        if step == 0:
            prepare()
            keep.wait()
            stage(me)
        else:
            if step > 1:
                at_distance(step - 1, staged)
            if step == 2:
                settle(me)
            if step > 2:
                at_distance(step - 2, settle)
    at_distance(count - 1, staged)
    if count == 2:
        settle(me)
    if count > 2:
        at_distance(count - 2, settle)
    at_distance(count - 1, settle)

    def drain():
        for step in range(count):
            low = me - step
            high = me + step

            @pl.when(jnp.logical_and(low >= 0, has_right))
            def _():
                hop(low, me + 1, step, send_right).wait_send()

            @pl.when(jnp.logical_and(high < count, has_left))
            def _():
                hop(high, me - 1, step, send_left).wait_send()

        for step in range(1, count):
            swap(lax.rem(me + step, count)).wait_send()

    return drain


def prepare_sketch(pattern_ref, contrib, assembled, columns_ref, targets_ref, held):
    pick, place, front, entries = held
    half = lax.axis_index("child")
    tile_rows, tile_cols = contrib.shape
    window_rows = assembled.shape[1]
    lanes = lax.broadcasted_iota(jnp.int32, (window_rows, tile_cols), 0)
    pick[...] = jnp.where(lanes == columns_ref[...], 1.0, 0.0).astype(jnp.bfloat16)
    rows = lax.broadcasted_iota(jnp.int32, (tile_rows, window_rows), 1)
    place[...] = jnp.where(rows == targets_ref[...], 1.0, 0.0).astype(jnp.bfloat16)
    front[0], front[1] = split(contrib[...])
    for row in range(tile_rows // BT):
        for col in range(window_rows // BT):
            where = (slice(row * BT, (row + 1) * BT), slice(col * BT, (col + 1) * BT))
            present = pattern_ref[half * (tile_rows // BT) + row, col].astype(jnp.float32)
            entries[(0,) + where], entries[(1,) + where] = split(assembled[where] * present)


def stacked(a, b, dims=NN):
    rows = a.shape[0] // 2
    both = dot16(a, b[0], dims)
    return both[:rows] + (dot16(a[:rows], b[1], dims) + both[rows:])


def sketch(omega, held, part_ref):
    pick, place, front, entries = held
    half = lax.axis_index("child")
    rows, tile_rows = omega.shape[0], place.shape[0]
    both = jnp.concatenate(split(omega), axis=0)
    picked = dot16(both, pick[...]).astype(jnp.bfloat16)
    product = stacked(picked, front, NT)
    sparse = stacked(both, entries, NT)
    spread = dot16(jnp.concatenate(split(product), axis=0), place[...])
    part_ref[...] = (spread[:rows] + spread[rows:]).reshape(part_ref.shape)
    where = pl.ds(pl.multiple_of(half * tile_rows, tile_rows), tile_rows)
    part_ref[:, :, :, where] = part_ref[:, :, :, where] + sparse.reshape(part_ref.shape[:3] + (tile_rows,))


class Reduce:
    def __init__(self, plane, part_ref, out_ref, pair_buf, sum_buf, chip_buf, sems):
        self.plane, self.part, self.out = plane, part_ref, out_ref
        self.pair_buf, self.sum_buf, self.chip_buf, self.sems = pair_buf, sum_buf, chip_buf, sems
        self.partner = plane.device(plane.chip, 1 - plane.core)

    def pair(self, r):
        source = self.part.at[r, :, 1 - self.plane.core]
        return remote(source, self.pair_buf.at[r], self.sems[0].at[r], self.sems[1].at[r], self.partner)

    def give(self, r, c):
        chip = self.plane.chip
        device = self.plane.device(c, self.plane.core)
        return remote(
            self.sum_buf.at[r, c], self.chip_buf.at[r, chip], self.sems[2].at[r, c], self.sems[3].at[r, chip], device
        )

    def take(self, r, c):
        device = self.plane.device(c, self.plane.core)
        return remote(self.sum_buf.at[r, c], self.chip_buf.at[r, c], self.sems[2].at[r, c], self.sems[3].at[r, c], device)

    def show(self, r, c, owner):
        block = self.out.at[r, owner, self.plane.core]
        device = self.plane.device(c, self.plane.core)
        return remote(block, block, self.sems[4].at[r, c], self.sems[5].at[r, owner], device)

    def hand(self, r, c, core):
        block = self.out.at[r, c, core]
        return remote(block, block, self.sems[6].at[r, c], self.sems[7].at[r, c], self.partner)

    def begin(self, r):
        self.pair(r).start()

    def settle(self, r):
        plane = self.plane
        self.pair(r).wait_recv()
        for c in plane.order[1:]:
            self.sum_buf[r, c] = self.part[r, c, plane.core] + self.pair_buf[r, c]
            self.give(r, c).start()

    def finish(self, stages):
        plane = self.plane
        chip, core, others = plane.chip, plane.core, plane.order[1:]
        for r in stages:
            total = self.part[r, chip, core] + self.pair_buf[r, chip]
            for c in others:
                self.take(r, c).wait_recv()
                total = total + self.chip_buf[r, c]
            self.out[r, chip, core] = total
            for c in others:
                self.show(r, c, chip).start()
            self.hand(r, chip, core).start()
        for r in stages:
            for c in others:
                self.show(r, c, c).wait_recv()
                self.hand(r, c, core).start()
        for r in stages:
            for c in plane.order:
                self.hand(r, c, 1 - core).wait_recv()

    def drain(self, stages):
        for r in stages:
            self.pair(r).wait_send()
            for c in self.plane.order[1:]:
                self.give(r, c).wait_send()
                self.show(r, c, self.plane.chip).wait_send()
            for c in self.plane.order:
                self.hand(r, c, self.plane.core).wait_send()


def eliminate(leaves):
    groups = NB // SUB
    index = lax.broadcasted_iota(jnp.int32, (SUB, 2 * NB), 0)
    wide = (SUB, 2 * NB)
    leaves = [list(rows) for rows in leaves]
    for panel in range(groups):
        first = panel * SUB
        columns = [
            {
                q: [jnp.broadcast_to(rows[q][:, first + k : first + k + 1], wide) for k in range(SUB)]
                for q in range(panel, groups)
            }
            for rows in leaves
        ]
        for k in range(SUB):
            for rows, cols in zip(leaves, columns):
                own = cols[panel]
                scale = lax.rsqrt(jnp.broadcast_to(own[k][k : k + 1], wide))
                pivot = jnp.broadcast_to(rows[panel][k : k + 1], wide) * scale
                weight = {q: cols[q][k] * scale for q in range(panel, groups)}
                across = weight[panel]
                below = jnp.where(index > k, across, 0.0)
                rows[panel] = jnp.where(index == k, pivot, rows[panel] - below * pivot)
                for j in range(k + 1, SUB):
                    factor = jnp.broadcast_to(across[j : j + 1], wide)
                    for q in range(panel, groups):
                        cols[q][j] = cols[q][j] - (below if q == panel else weight[q]) * factor
                for q in range(panel + 1, groups):
                    rows[q] = rows[q] - weight[q] * pivot
    return leaves


def factor(bound, window, work, done_block):
    columns, window_rows = window.shape
    top = window_rows // 2 + window_rows // 16
    low = window_rows // 2 - window_rows // 16
    eye = jnp.where(
        lax.broadcasted_iota(jnp.int32, (columns, columns), 0)
        == lax.broadcasted_iota(jnp.int32, (columns, columns), 1),
        1.0,
        0.0,
    )
    lane = lax.broadcasted_iota(jnp.int32, (columns, window_rows), 1)
    head = jnp.where(lane < bound, window, 0.0)
    tail = window - head
    spans = ((head, 0, (top + 127) // 128 * 128), (tail, low // 128 * 128, window_rows))
    counts = (bound, window_rows - bound)
    for leaf, (masked, start, stop) in enumerate(spans):
        part = masked[:, start:stop]
        gram = mm3(part, part, NT)
        work[leaf, :, :columns] = gram / counts[leaf].astype(jnp.float32)
        work[leaf, :, columns:] = eye
    small_eye = eye[:NB, :NB]
    for block in range(columns // NB):
        begin, end = block * NB, (block + 1) * NB
        aug = []
        for leaf in range(2):
            diagonal = jnp.concatenate([work[leaf, begin:end, begin:end], small_eye], axis=1)
            aug.append([diagonal[q * SUB : (q + 1) * SUB] for q in range(NB // SUB)])
        done = eliminate(aug)
        for leaf in range(2):
            inverse = jnp.concatenate(done[leaf], axis=0)[:, NB:]
            rows = mm(inverse, work[leaf, begin:end, :])
            work[leaf, begin:end, :] = rows
            done_block(leaf, block, begin, end, rows[:, :columns])
            if end < columns:
                work[leaf, end:, :] = work[leaf, end:, :] - mm3(rows[:, end:columns], rows, TN)


def whole_kernel(
    bound_ref, pattern_ref, omega_ref, contrib_ref, assembled_ref, columns_ref, targets_ref, bases_ref, coupling_ref,
    gathered, contrib_buf, assembled_buf, pick, place, front, entries,
    part, window, pair_buf, sum_buf, chip_buf, work, upper, sibling, input_sems, *sems,
):
    plane = Plane()
    window_rows = assembled_buf.shape[1]
    columns, width = upper.shape[1], bases_ref.shape[0]
    held = (pick, place, front, entries)
    load_front = pltpu.make_async_copy(contrib_ref.at[0], contrib_buf, input_sems.at[0])
    load_entries = pltpu.make_async_copy(assembled_ref.at[0], assembled_buf, input_sems.at[1])
    load_front.start()
    load_entries.start()
    greet(plane)

    def prepare():
        load_front.wait()
        load_entries.wait()
        prepare_sketch(pattern_ref, contrib_buf, assembled_buf, columns_ref, targets_ref, held)

    stages = part.shape[0]
    row_count, row_pos = lax.axis_size("row"), lax.axis_index("row")
    summing = Reduce(plane, part, window, pair_buf, sum_buf, chip_buf, sems[6:14])
    if stages == row_count:

        def stage(block):
            sketch(gathered[block].reshape(columns // stages, window_rows), held, part.at[block])
            summing.begin(block)

        drain_gather = gather(omega_ref, gathered, sems[:6], prepare, stage, summing.settle)
        order = [lax.rem(row_pos + step, row_count) for step in range(row_count)]
    else:
        drain_gather = gather(omega_ref, gathered, sems[:6], prepare, lambda block: None, lambda block: None)
        sketch(gathered[...].reshape(columns, window_rows), held, part.at[0])
        summing.begin(0)
        summing.settle(0)
        order = [0]
    summing.finish(order)
    drain_gather()
    summing.drain(order)

    near_send, near_recv = sems[14:]
    near = {"row": row_pos + 1 - 2 * (row_pos % 2)}

    def send(leaf, block):
        start = block * NB // 128 * 128
        rows = slice(block * NB, (block + 1) * NB)
        source, target = upper.at[leaf, rows, start:], sibling.at[leaf, rows, start:]
        return remote(source, target, near_send.at[leaf, block], near_recv.at[leaf, block], near)

    def done_block(leaf, block, begin, end, rows):
        keep = lax.broadcasted_iota(jnp.int32, rows.shape, 1) >= begin + lax.broadcasted_iota(
            jnp.int32, rows.shape, 0
        )
        upper[leaf, begin:end, :] = jnp.where(keep, rows, 0.0)
        send(leaf, block).start()

    bound = bound_ref[0]
    samples = window[...].reshape(columns, window_rows)
    factor(bound, samples, work, done_block)
    mine = pl.ds(pl.multiple_of(plane.group * width, width), width)
    inverse = jnp.concatenate([work[0, mine, columns:], work[1, mine, columns:]], axis=0)
    both = mm3(inverse, samples)
    lane = lax.broadcasted_iota(jnp.int32, (width, window_rows), 1)
    bases_ref[...] = jnp.where(lane < bound, both[:width], both[width:])
    for leaf in range(2):
        own = upper[leaf, mine, :]
        pieces = []
        for block in range(columns // NB):
            start = block * NB // 128 * 128
            send(leaf, block).wait_recv()
            pieces.append(mm3(own[:, start:], sibling[leaf, block * NB : (block + 1) * NB, start:], NT))
        coupling_ref[0, leaf] = jnp.concatenate(pieces, axis=1)
    for leaf in range(2):
        for block in range(columns // NB):
            send(leaf, block).wait_send()


def local(contrib, assembled, pattern, omega, row_maps, leaf_bounds):
    tile_rows, tile_cols = contrib.shape[1:]
    window_rows, own_width = omega.shape
    rows = lax.axis_size("row")
    chips = lax.axis_size("col") * lax.axis_size("child") // 2
    columns = own_width * rows
    width = columns // (2 * chips)
    row_pos = lax.axis_index("row")
    col_pos = lax.axis_index("col")
    child_maps = row_maps[0]
    col_maps = lax.dynamic_slice_in_dim(child_maps, col_pos * tile_cols, tile_cols) - col_pos * window_rows
    targets = lax.dynamic_slice_in_dim(child_maps, row_pos * tile_rows, tile_rows) - row_pos * window_rows
    own = omega.T.reshape(2, own_width // 2, window_rows)
    f32, bf16, dma = jnp.float32, jnp.bfloat16, pltpu.SemaphoreType.DMA
    any_space = pl.BlockSpec(memory_space=pl.ANY)
    stages = rows if columns // (rows * 2 * chips) >= SUB else 1
    piece = width // stages
    block = pltpu.VMEM((stages, chips, piece, window_rows), f32)
    split_window = pltpu.VMEM((stages, chips, 2, piece, window_rows), f32)
    bases, coupling = pl.pallas_call(
        whole_kernel,
        out_shape=(
            jax.ShapeDtypeStruct((width, window_rows), f32),
            jax.ShapeDtypeStruct((1, 2, width, columns), f32),
        ),
        in_specs=[SMEM, SMEM, VMEM, any_space, any_space, VMEM, VMEM],
        out_specs=(VMEM, VMEM),
        scratch_shapes=[
            pltpu.VMEM((rows, 2, own_width // 2, window_rows), f32),
            pltpu.VMEM((tile_rows, tile_cols), f32),
            pltpu.VMEM((tile_rows, window_rows), f32),
            pltpu.VMEM((window_rows, tile_cols), bf16),
            pltpu.VMEM((tile_rows, window_rows), bf16),
            pltpu.VMEM((2, tile_rows, tile_cols), bf16),
            pltpu.VMEM((2, tile_rows, window_rows), bf16),
            split_window,
            split_window,
            block,
            block,
            block,
            pltpu.VMEM((2, columns, 2 * columns), f32),
            pltpu.VMEM((2, columns, columns), f32),
            pltpu.VMEM((2, columns, columns), f32),
            dma((2,)),
        ]
        + [dma((rows,))] * 5
        + [dma]
        + [dma((stages,))] * 2
        + [dma((stages, chips))] * 6
        + [dma((2, columns // NB))] * 2,
        compiler_params=pltpu.CompilerParams(
            collective_id=0, has_side_effects=True, vmem_limit_bytes=56 << 20
        ),
        name="front_samples",
    )(leaf_bounds, pattern, own, contrib, assembled, col_maps[None, :], targets[:, None])
    return (bases.T, coupling)


def solution(mesh):
    in_specs = (
        P("child", "row", "col"),
        P("child", "row", "col"),
        P("row", "col"),
        P("col", "row"),
        P("child", None),
        P("row"),
    )
    out_specs = (P("row", ("child", "col")), P("row", None, ("child", "col"), None))
    return jax.shard_map(local, mesh=mesh, in_specs=in_specs, out_specs=out_specs, check_vma=False)
```

```python
import jax
import jax.numpy as jnp
from jax import lax
from jax.experimental import pallas as pl
from jax.experimental.pallas import tpu as pltpu
from jax.sharding import PartitionSpec as P

BT = 256
NB = 64
SUB = 8
MESH = pl.DeviceIdType.MESH
VMEM = pl.BlockSpec(memory_space=pltpu.VMEM)
SMEM = pl.BlockSpec(memory_space=pltpu.SMEM)

NN = (((1,), (0,)), ((), ()))
NT = (((1,), (1,)), ((), ()))
TN = (((0,), (0,)), ((), ()))


def split(a):
    high = a.astype(jnp.bfloat16)
    low = (a - high.astype(jnp.float32)).astype(jnp.bfloat16)
    return high, low


def dot16(a, b, dims=NN):
    return lax.dot_general(a, b, dims, preferred_element_type=jnp.float32)


def mm3(a, b, dims=NN):
    (ah, al), (bh, bl) = split(a), split(b)
    return dot16(ah, bh, dims) + (dot16(ah, bl, dims) + dot16(al, bh, dims))


class Plane:
    def __init__(self):
        self.cols = lax.axis_size("col")
        self.chips = self.cols * lax.axis_size("child") // 2
        self.group = lax.axis_index("child") * self.cols + lax.axis_index("col")
        self.chip = self.group // 2
        self.core = self.group % 2
        self.order = [lax.rem(self.chip + step, self.chips) for step in range(self.chips)]

    def device(self, chip, core):
        flat = chip * 2 + core
        return {"child": flat // self.cols, "col": flat % self.cols}


def remote(source, target, send_sem, recv_sem, device):
    return pltpu.make_async_remote_copy(
        src_ref=source, dst_ref=target, send_sem=send_sem, recv_sem=recv_sem, device_id=device, device_id_type=MESH
    )


def greet(plane):
    count = lax.axis_size("row")
    me = lax.axis_index("row")
    barrier = pltpu.get_barrier_semaphore()

    @pl.when(me > 0)
    def _():
        pl.semaphore_signal(barrier, inc=1, device_id={"row": me - 1}, device_id_type=MESH)

    @pl.when(me < count - 1)
    def _():
        pl.semaphore_signal(barrier, inc=1, device_id={"row": me + 1}, device_id_type=MESH)

    pl.semaphore_signal(barrier, inc=1, device_id=plane.device(plane.chip, 1 - plane.core), device_id_type=MESH)
    for step in range(1, plane.chips):
        pl.semaphore_signal(
            barrier, inc=1, device_id=plane.device(plane.order[step], plane.core), device_id_type=MESH
        )
    pl.semaphore_wait(barrier, plane.chips + jnp.minimum(me, 1) + jnp.minimum(count - 1 - me, 1))


def gather(own_ref, out_ref, sems, prepare, stage, settle, finalize):
    send_right, send_left, recv, swap_send, swap_recv, local_sem = sems
    count = lax.axis_size("row")
    me = lax.axis_index("row")
    half = lax.axis_index("child")
    has_left = me > 0
    has_right = me < count - 1
    keep = pltpu.make_async_copy(own_ref, out_ref.at[me], local_sem)
    keep.start()

    def hop(block, target, step, send):
        source = own_ref.at[half] if step == 0 else out_ref.at[block, half]
        return remote(source, out_ref.at[block, half], send.at[block], recv.at[block], {"row": target})

    def swap(block):
        place = out_ref.at[block, half]
        return remote(place, place, swap_send.at[block], swap_recv.at[block], {"child": 1 - half})

    def at_distance(step, act):
        for block, there in ((me - step, me >= step), (me + step, me + step < count)):

            @pl.when(there)
            def _():
                act(block)

    def wait_swap(block):
        place = out_ref.at[block, 1 - half]
        remote(place, place, swap_send.at[block], swap_recv.at[block], {"child": 1 - half}).wait_recv()

    def staged(block):
        wait_swap(block)
        stage(block)

    for step in range(count):
        low = me - step
        high = me + step
        if step > 0:

            @pl.when(low >= 0)
            def _():
                hop(low, me - 1, step, send_right).wait_recv()

        @pl.when(jnp.logical_and(low >= 0, has_right))
        def _():
            hop(low, me + 1, step, send_right).start()

        if step > 0:

            @pl.when(low >= 0)
            def _():
                swap(low).start()

            @pl.when(high < count)
            def _():
                hop(high, me + 1, step, send_left).wait_recv()

        @pl.when(jnp.logical_and(high < count, has_left))
        def _():
            hop(high, me - 1, step, send_left).start()

        if step > 0:

            @pl.when(high < count)
            def _():
                swap(high).start()

        if step == 0:
            prepare()
            keep.wait()
            stage(me)
        else:
            if step > 1:
                at_distance(step - 1, staged)
            if step == 2:
                settle(me)
            if step > 2:
                at_distance(step - 2, settle)
            if step == 3:
                finalize(me)
            if step > 3:
                at_distance(step - 3, finalize)
    at_distance(count - 1, staged)
    if count == 2:
        settle(me)
    if count > 2:
        at_distance(count - 2, settle)
    if count < 4:
        finalize(me)
    for step in range(max(count - 3, 1), count - 1):
        at_distance(step, finalize)
    at_distance(count - 1, settle)
    at_distance(count - 1, finalize)

    def drain():
        for step in range(count):
            low = me - step
            high = me + step

            @pl.when(jnp.logical_and(low >= 0, has_right))
            def _():
                hop(low, me + 1, step, send_right).wait_send()

            @pl.when(jnp.logical_and(high < count, has_left))
            def _():
                hop(high, me - 1, step, send_left).wait_send()

        for step in range(1, count):
            swap(lax.rem(me + step, count)).wait_send()

    def nearest(act):
        act(me)
        for step in range(1, count):
            at_distance(step, act)

    return drain, nearest


def prepare_sketch(pattern_ref, contrib, assembled, maps_ref, held):
    pick, place, front, entries = held
    half = lax.axis_index("child")
    tile_rows, tile_cols = contrib.shape
    window_rows = assembled.shape[1]
    row_pos, col_pos = lax.axis_index("row"), lax.axis_index("col")
    columns = maps_ref[:, pl.ds(pl.multiple_of(col_pos * tile_cols, tile_cols), tile_cols)] - col_pos * window_rows
    targets = maps_ref[:, pl.ds(pl.multiple_of(row_pos * tile_rows, tile_rows), tile_rows)] - row_pos * window_rows
    index = lax.broadcasted_iota(jnp.int32, (window_rows, tile_cols), 0)
    pick[...] = jnp.where(index == columns, 1.0, 0.0).astype(jnp.bfloat16)
    index = lax.broadcasted_iota(jnp.int32, (window_rows, tile_rows), 0)
    place[...] = jnp.where(index == targets, 1.0, 0.0).astype(jnp.bfloat16)
    front[0], front[1] = split(contrib[...])
    for row in range(tile_rows // BT):
        for col in range(window_rows // BT):
            where = (slice(row * BT, (row + 1) * BT), slice(col * BT, (col + 1) * BT))
            present = pattern_ref[half * (tile_rows // BT) + row, col].astype(jnp.float32)
            entries[(0,) + where], entries[(1,) + where] = split(assembled[where] * present)


def stacked(a, b, dims=NN):
    rows = a.shape[0] // 2
    both = dot16(a, b[0], dims)
    return both[:rows] + (dot16(a[:rows], b[1], dims) + both[rows:])


def sketch(omega, held, part_ref):
    pick, place, front, entries = held
    half = lax.axis_index("child")
    rows, tile_rows = omega.shape[0], place.shape[1]
    both = jnp.concatenate(split(omega), axis=0)
    picked = dot16(both, pick[...]).astype(jnp.bfloat16)
    product = stacked(picked, front, NT)
    sparse = stacked(both, entries, NT)
    spread = dot16(jnp.concatenate(split(product), axis=0), place[...], NT)
    part_ref[...] = (spread[:rows] + spread[rows:]).reshape(part_ref.shape)
    where = pl.ds(pl.multiple_of(half * tile_rows, tile_rows), tile_rows)
    part_ref[:, :, :, where] = part_ref[:, :, :, where] + sparse.reshape(part_ref.shape[:3] + (tile_rows,))


class Reduce:
    def __init__(self, plane, part_ref, out_ref, pair_buf, sum_buf, chip_buf, sems):
        self.plane, self.part, self.out = plane, part_ref, out_ref
        self.pair_buf, self.sum_buf, self.chip_buf, self.sems = pair_buf, sum_buf, chip_buf, sems
        self.partner = plane.device(plane.chip, 1 - plane.core)

    def pair(self, r):
        source = self.part.at[r, :, 1 - self.plane.core]
        return remote(source, self.pair_buf.at[r], self.sems[0].at[r], self.sems[1].at[r], self.partner)

    def give(self, r, c):
        chip = self.plane.chip
        device = self.plane.device(c, self.plane.core)
        return remote(
            self.sum_buf.at[r, c], self.chip_buf.at[r, chip], self.sems[2].at[r, c], self.sems[3].at[r, chip], device
        )

    def take(self, r, c):
        device = self.plane.device(c, self.plane.core)
        return remote(self.sum_buf.at[r, c], self.chip_buf.at[r, c], self.sems[2].at[r, c], self.sems[3].at[r, c], device)

    def show(self, r, c, owner):
        block = self.out.at[r, owner, self.plane.core]
        device = self.plane.device(c, self.plane.core)
        return remote(block, block, self.sems[4].at[r, c], self.sems[5].at[r, owner], device)

    def hand(self, r, c, core):
        block = self.out.at[r, c, core]
        return remote(block, block, self.sems[6].at[r, c], self.sems[7].at[r, c], self.partner)

    def begin(self, r):
        self.pair(r).start()

    def settle(self, r):
        plane = self.plane
        self.pair(r).wait_recv()
        for c in plane.order[1:]:
            self.sum_buf[r, c] = self.part[r, c, plane.core] + self.pair_buf[r, c]
            self.give(r, c).start()

    def finalize(self, r):
        plane = self.plane
        chip, core, others = plane.chip, plane.core, plane.order[1:]
        total = self.part[r, chip, core] + self.pair_buf[r, chip]
        for c in others:
            self.take(r, c).wait_recv()
            total = total + self.chip_buf[r, c]
        self.out[r, chip, core] = total
        for c in others:
            self.show(r, c, chip).start()
        self.hand(r, chip, core).start()

    def forward(self, r):
        for c in self.plane.order[1:]:
            self.show(r, c, c).wait_recv()
            self.hand(r, c, self.plane.core).start()

    def arrive(self, r):
        for c in self.plane.order:
            self.hand(r, c, 1 - self.plane.core).wait_recv()

    def drain(self, stages):
        for r in stages:
            self.pair(r).wait_send()
            for c in self.plane.order[1:]:
                self.give(r, c).wait_send()
                self.show(r, c, self.plane.chip).wait_send()
            for c in self.plane.order:
                self.hand(r, c, self.plane.core).wait_send()


def eliminate(leaves):
    groups = NB // SUB
    index = lax.broadcasted_iota(jnp.int32, (SUB, 2 * NB), 0)
    wide = (SUB, 2 * NB)
    leaves = [list(rows) for rows in leaves]
    for panel in range(groups):
        first = panel * SUB
        columns = [
            {
                q: [jnp.broadcast_to(rows[q][:, first + k : first + k + 1], wide) for k in range(SUB)]
                for q in range(panel, groups)
            }
            for rows in leaves
        ]
        for k in range(SUB):
            for rows, cols in zip(leaves, columns):
                own = cols[panel]
                scale = lax.rsqrt(jnp.broadcast_to(own[k][k : k + 1], wide))
                pivot = jnp.broadcast_to(rows[panel][k : k + 1], wide) * scale
                weight = {q: cols[q][k] * scale for q in range(panel, groups)}
                across = weight[panel]
                below = jnp.where(index > k, across, 0.0)
                rows[panel] = jnp.where(index == k, pivot, rows[panel] - below * pivot)
                for j in range(k + 1, SUB):
                    factor = jnp.broadcast_to(across[j : j + 1], wide)
                    for q in range(panel, groups):
                        cols[q][j] = cols[q][j] - (below if q == panel else weight[q]) * factor
                for q in range(panel + 1, groups):
                    rows[q] = rows[q] - weight[q] * pivot
    return leaves


def factor(bound, window, work, done_block):
    columns, window_rows = window.shape
    top = window_rows // 2 + window_rows // 16
    low = window_rows // 2 - window_rows // 16
    eye = jnp.where(
        lax.broadcasted_iota(jnp.int32, (columns, columns), 0)
        == lax.broadcasted_iota(jnp.int32, (columns, columns), 1),
        1.0,
        0.0,
    )
    lane = lax.broadcasted_iota(jnp.int32, (columns, window_rows), 1)
    head = jnp.where(lane < bound, window, 0.0)
    tail = window - head
    spans = ((head, 0, (top + 127) // 128 * 128), (tail, low // 128 * 128, window_rows))
    counts = (bound, window_rows - bound)
    for leaf, (masked, start, stop) in enumerate(spans):
        part = masked[:, start:stop]
        gram = mm3(part, part, NT)
        work[leaf, :, :columns] = gram / counts[leaf].astype(jnp.float32)
        work[leaf, :, columns:] = eye
    small_eye = eye[:NB, :NB]
    for block in range(columns // NB):
        begin, end = block * NB, (block + 1) * NB
        aug = []
        for leaf in range(2):
            diagonal = jnp.concatenate([work[leaf, begin:end, begin:end], small_eye], axis=1)
            aug.append([diagonal[q * SUB : (q + 1) * SUB] for q in range(NB // SUB)])
        done = eliminate(aug)
        for leaf in range(2):
            inverse = jnp.concatenate(done[leaf], axis=0)[:, NB:]
            rows = mm3(inverse, work[leaf, begin:end, :])
            work[leaf, begin:end, :] = rows
            done_block(leaf, block, begin, end, rows[:, :columns])
            if end < columns:
                work[leaf, end:, :] = work[leaf, end:, :] - mm3(rows[:, end:columns], rows, TN)


def whole_kernel(
    bound_ref, pattern_ref, omega_ref, contrib_ref, assembled_ref, maps_ref, bases_ref, coupling_ref,
    gathered, contrib_buf, assembled_buf, pick, place, front, entries,
    part, window, pair_buf, sum_buf, chip_buf, work, upper, sibling, input_sems, *sems,
):
    plane = Plane()
    window_rows = assembled_buf.shape[1]
    columns, width = upper.shape[1], bases_ref.shape[0]
    held = (pick, place, front, entries)
    load_front = pltpu.make_async_copy(contrib_ref.at[0], contrib_buf, input_sems.at[0])
    load_entries = pltpu.make_async_copy(assembled_ref.at[0], assembled_buf, input_sems.at[1])
    load_front.start()
    load_entries.start()
    greet(plane)

    def prepare():
        load_front.wait()
        load_entries.wait()
        prepare_sketch(pattern_ref, contrib_buf, assembled_buf, maps_ref, held)

    stages = part.shape[0]
    row_count, row_pos = lax.axis_size("row"), lax.axis_index("row")
    summing = Reduce(plane, part, window, pair_buf, sum_buf, chip_buf, sems[6:14])
    if stages == row_count:

        def stage(block):
            sketch(gathered[block].reshape(columns // stages, window_rows), held, part.at[block])
            summing.begin(block)

        drain_gather, nearest = gather(
            omega_ref, gathered, sems[:6], prepare, stage, summing.settle, summing.finalize
        )
        nearest(summing.forward)
        order = [lax.rem(row_pos + step, row_count) for step in range(row_count)]
    else:
        idle = lambda block: None
        drain_gather, nearest = gather(omega_ref, gathered, sems[:6], prepare, idle, idle, idle)
        sketch(gathered[...].reshape(columns, window_rows), held, part.at[0])
        summing.begin(0)
        summing.settle(0)
        summing.finalize(0)
        summing.forward(0)
        order = [0]
    for r in order:
        summing.arrive(r)
    drain_gather()
    summing.drain(order)

    near_send, near_recv = sems[14:]
    near = {"row": row_pos + 1 - 2 * (row_pos % 2)}

    def send(leaf, block):
        start = block * NB // 128 * 128
        rows = slice(block * NB, (block + 1) * NB)
        source, target = upper.at[leaf, rows, start:], sibling.at[leaf, rows, start:]
        return remote(source, target, near_send.at[leaf, block], near_recv.at[leaf, block], near)

    def done_block(leaf, block, begin, end, rows):
        keep = lax.broadcasted_iota(jnp.int32, rows.shape, 1) >= begin + lax.broadcasted_iota(
            jnp.int32, rows.shape, 0
        )
        upper[leaf, begin:end, :] = jnp.where(keep, rows, 0.0)
        send(leaf, block).start()

    bound = bound_ref[0]
    samples = window[...].reshape(columns, window_rows)
    factor(bound, samples, work, done_block)
    mine = pl.ds(pl.multiple_of(plane.group * width, width), width)
    inverse = jnp.concatenate([work[0, mine, columns:], work[1, mine, columns:]], axis=0)
    both = mm3(inverse, samples)
    lane = lax.broadcasted_iota(jnp.int32, (width, window_rows), 1)
    bases_ref[...] = jnp.where(lane < bound, both[:width], both[width:])
    for leaf in range(2):
        own = upper[leaf, mine, :]
        pieces = []
        for block in range(columns // NB):
            start = block * NB // 128 * 128
            send(leaf, block).wait_recv()
            pieces.append(mm3(own[:, start:], sibling[leaf, block * NB : (block + 1) * NB, start:], NT))
        coupling_ref[0, leaf] = jnp.concatenate(pieces, axis=1)
    for leaf in range(2):
        for block in range(columns // NB):
            send(leaf, block).wait_send()


def deliver_kernel(bases_ref, coupling_ref, bases_out, coupling_out):
    bases_out[...] = bases_ref[...]
    coupling_out[...] = coupling_ref[...]


def local(contrib, assembled, pattern, omega, row_maps, leaf_bounds):
    tile_rows, tile_cols = contrib.shape[1:]
    window_rows, own_width = omega.shape
    rows = lax.axis_size("row")
    chips = lax.axis_size("col") * lax.axis_size("child") // 2
    columns = own_width * rows
    width = columns // (2 * chips)
    own = omega.T.reshape(2, own_width // 2, window_rows)
    f32, bf16, dma = jnp.float32, jnp.bfloat16, pltpu.SemaphoreType.DMA
    any_space = pl.BlockSpec(memory_space=pl.ANY)
    stages = rows if columns // (rows * 2 * chips) >= SUB else 1
    piece = width // stages
    block = pltpu.VMEM((stages, chips, piece, window_rows), f32)
    split_window = pltpu.VMEM((stages, chips, 2, piece, window_rows), f32)
    bases, coupling = pl.pallas_call(
        whole_kernel,
        out_shape=(
            jax.ShapeDtypeStruct((width, window_rows), f32),
            jax.ShapeDtypeStruct((1, 2, width, columns), f32),
        ),
        in_specs=[SMEM, SMEM, VMEM, any_space, any_space, VMEM],
        out_specs=(VMEM, VMEM),
        scratch_shapes=[
            pltpu.VMEM((rows, 2, own_width // 2, window_rows), f32),
            pltpu.VMEM((tile_rows, tile_cols), f32),
            pltpu.VMEM((tile_rows, window_rows), f32),
            pltpu.VMEM((window_rows, tile_cols), bf16),
            pltpu.VMEM((window_rows, tile_rows), bf16),
            pltpu.VMEM((2, tile_rows, tile_cols), bf16),
            pltpu.VMEM((2, tile_rows, window_rows), bf16),
            split_window,
            split_window,
            block,
            block,
            block,
            pltpu.VMEM((2, columns, 2 * columns), f32),
            pltpu.VMEM((2, columns, columns), f32),
            pltpu.VMEM((2, columns, columns), f32),
            dma((2,)),
        ]
        + [dma((rows,))] * 5
        + [dma]
        + [dma((stages,))] * 2
        + [dma((stages, chips))] * 6
        + [dma((2, columns // NB))] * 2,
        compiler_params=pltpu.CompilerParams(
            collective_id=0, has_side_effects=True, vmem_limit_bytes=56 << 20
        ),
        name="front_samples",
    )(leaf_bounds, pattern, own, contrib, assembled, row_maps)
    bases, coupling = pl.pallas_call(
        deliver_kernel,
        out_shape=(
            jax.ShapeDtypeStruct(bases.shape, f32),
            jax.ShapeDtypeStruct(coupling.shape, f32),
        ),
        in_specs=[VMEM, VMEM],
        out_specs=(VMEM, VMEM),
        name="deliver",
    )(bases, coupling)
    return (bases.T, coupling)


def solution(mesh):
    in_specs = (
        P("child", "row", "col"),
        P("child", "row", "col"),
        P("row", "col"),
        P("col", "row"),
        P("child", None),
        P("row"),
    )
    out_specs = (P("row", ("child", "col")), P("row", None, ("child", "col"), None))
    return jax.shard_map(local, mesh=mesh, in_specs=in_specs, out_specs=out_specs, check_vma=False)
```

```python
import jax
import jax.numpy as jnp
from jax import lax
from jax.experimental import pallas as pl
from jax.experimental.pallas import tpu as pltpu
from jax.sharding import PartitionSpec as P

BT = 256
NB = 64
SUB = 8
MESH = pl.DeviceIdType.MESH
VMEM = pl.BlockSpec(memory_space=pltpu.VMEM)
SMEM = pl.BlockSpec(memory_space=pltpu.SMEM)

NN = (((1,), (0,)), ((), ()))
NT = (((1,), (1,)), ((), ()))
TN = (((0,), (0,)), ((), ()))


def split(a):
    high = a.astype(jnp.bfloat16)
    low = (a - high.astype(jnp.float32)).astype(jnp.bfloat16)
    return high, low


def dot16(a, b, dims=NN):
    return lax.dot_general(a, b, dims, preferred_element_type=jnp.float32)


def mm3(a, b, dims=NN):
    (ah, al), (bh, bl) = split(a), split(b)
    return dot16(ah, bh, dims) + (dot16(ah, bl, dims) + dot16(al, bh, dims))


class Plane:
    def __init__(self):
        self.cols = lax.axis_size("col")
        self.chips = self.cols * lax.axis_size("child") // 2
        self.group = lax.axis_index("child") * self.cols + lax.axis_index("col")
        self.chip = self.group // 2
        self.core = self.group % 2
        self.order = [lax.rem(self.chip + step, self.chips) for step in range(self.chips)]

    def device(self, chip, core):
        flat = chip * 2 + core
        return {"child": flat // self.cols, "col": flat % self.cols}


def remote(source, target, send_sem, recv_sem, device):
    return pltpu.make_async_remote_copy(
        src_ref=source, dst_ref=target, send_sem=send_sem, recv_sem=recv_sem, device_id=device, device_id_type=MESH
    )


def greet(plane):
    count = lax.axis_size("row")
    me = lax.axis_index("row")
    barrier = pltpu.get_barrier_semaphore()

    @pl.when(me > 0)
    def _():
        pl.semaphore_signal(barrier, inc=1, device_id={"row": me - 1}, device_id_type=MESH)

    @pl.when(me < count - 1)
    def _():
        pl.semaphore_signal(barrier, inc=1, device_id={"row": me + 1}, device_id_type=MESH)

    pl.semaphore_signal(barrier, inc=1, device_id=plane.device(plane.chip, 1 - plane.core), device_id_type=MESH)
    for step in range(1, plane.chips):
        pl.semaphore_signal(
            barrier, inc=1, device_id=plane.device(plane.order[step], plane.core), device_id_type=MESH
        )
    pl.semaphore_wait(barrier, plane.chips + jnp.minimum(me, 1) + jnp.minimum(count - 1 - me, 1))


def gather(own_ref, out_ref, sems, prepare, stage, settle, finalize):
    send_right, send_left, recv, swap_send, swap_recv, local_sem = sems
    count = lax.axis_size("row")
    me = lax.axis_index("row")
    half = lax.axis_index("child")
    has_left = me > 0
    has_right = me < count - 1
    keep = pltpu.make_async_copy(own_ref, out_ref.at[me], local_sem)
    keep.start()

    def hop(block, target, step, send):
        source = own_ref.at[half] if step == 0 else out_ref.at[block, half]
        return remote(source, out_ref.at[block, half], send.at[block], recv.at[block], {"row": target})

    def swap(block):
        place = out_ref.at[block, half]
        return remote(place, place, swap_send.at[block], swap_recv.at[block], {"child": 1 - half})

    def at_distance(step, act):
        for block, there in ((me - step, me >= step), (me + step, me + step < count)):

            @pl.when(there)
            def _():
                act(block)

    def wait_swap(block):
        place = out_ref.at[block, 1 - half]
        remote(place, place, swap_send.at[block], swap_recv.at[block], {"child": 1 - half}).wait_recv()

    def staged(block):
        wait_swap(block)
        stage(block)

    for step in range(count):
        low = me - step
        high = me + step
        if step > 0:

            @pl.when(low >= 0)
            def _():
                hop(low, me - 1, step, send_right).wait_recv()

        @pl.when(jnp.logical_and(low >= 0, has_right))
        def _():
            hop(low, me + 1, step, send_right).start()

        if step > 0:

            @pl.when(low >= 0)
            def _():
                swap(low).start()

            @pl.when(high < count)
            def _():
                hop(high, me + 1, step, send_left).wait_recv()

        @pl.when(jnp.logical_and(high < count, has_left))
        def _():
            hop(high, me - 1, step, send_left).start()

        if step > 0:

            @pl.when(high < count)
            def _():
                swap(high).start()

        if step == 0:
            prepare()
            keep.wait()
            stage(me)
        else:
            if step > 1:
                at_distance(step - 1, staged)
            if step == 2:
                settle(me)
            if step > 2:
                at_distance(step - 2, settle)
            if step == 3:
                finalize(me)
            if step > 3:
                at_distance(step - 3, finalize)
    at_distance(count - 1, staged)
    if count == 2:
        settle(me)
    if count > 2:
        at_distance(count - 2, settle)
    if count < 4:
        finalize(me)
    for step in range(max(count - 3, 1), count - 1):
        at_distance(step, finalize)
    at_distance(count - 1, settle)
    at_distance(count - 1, finalize)

    def drain():
        for step in range(count):
            low = me - step
            high = me + step

            @pl.when(jnp.logical_and(low >= 0, has_right))
            def _():
                hop(low, me + 1, step, send_right).wait_send()

            @pl.when(jnp.logical_and(high < count, has_left))
            def _():
                hop(high, me - 1, step, send_left).wait_send()

        for step in range(1, count):
            swap(lax.rem(me + step, count)).wait_send()

    def nearest(act):
        act(me)
        for step in range(1, count):
            at_distance(step, act)

    return drain, nearest


def prepare_sketch(pattern_ref, contrib, assembled, maps_ref, held):
    pick, place, front, entries = held
    half = lax.axis_index("child")
    tile_rows, tile_cols = contrib.shape
    window_rows = assembled.shape[1]
    row_pos, col_pos = lax.axis_index("row"), lax.axis_index("col")
    columns = maps_ref[:, pl.ds(pl.multiple_of(col_pos * tile_cols, tile_cols), tile_cols)] - col_pos * window_rows
    targets = maps_ref[:, pl.ds(pl.multiple_of(row_pos * tile_rows, tile_rows), tile_rows)] - row_pos * window_rows
    index = lax.broadcasted_iota(jnp.int32, (window_rows, tile_cols), 0)
    pick[...] = jnp.where(index == columns, 1.0, 0.0).astype(jnp.bfloat16)
    index = lax.broadcasted_iota(jnp.int32, (window_rows, tile_rows), 0)
    place[...] = jnp.where(index == targets, 1.0, 0.0).astype(jnp.bfloat16)
    front[0], front[1] = split(contrib[...])
    for row in range(tile_rows // BT):
        for col in range(window_rows // BT):
            where = (slice(row * BT, (row + 1) * BT), slice(col * BT, (col + 1) * BT))
            present = pattern_ref[half * (tile_rows // BT) + row, col].astype(jnp.float32)
            entries[(0,) + where], entries[(1,) + where] = split(assembled[where] * present)


def stacked(a, b, dims=NN):
    rows = a.shape[0] // 2
    both = dot16(a, b[0], dims)
    return both[:rows] + (dot16(a[:rows], b[1], dims) + both[rows:])


def sketch(omega, held, part_ref):
    pick, place, front, entries = held
    half = lax.axis_index("child")
    rows, tile_rows = omega.shape[0], place.shape[1]
    both = jnp.concatenate(split(omega), axis=0)
    picked = dot16(both, pick[...]).astype(jnp.bfloat16)
    product = stacked(picked, front, NT)
    sparse = stacked(both, entries, NT)
    spread = dot16(jnp.concatenate(split(product), axis=0), place[...], NT)
    part_ref[...] = (spread[:rows] + spread[rows:]).reshape(part_ref.shape)
    where = pl.ds(pl.multiple_of(half * tile_rows, tile_rows), tile_rows)
    part_ref[:, :, :, where] = part_ref[:, :, :, where] + sparse.reshape(part_ref.shape[:3] + (tile_rows,))


class Reduce:
    def __init__(self, plane, part_ref, out_ref, pair_buf, sum_buf, chip_buf, sems):
        self.plane, self.part, self.out = plane, part_ref, out_ref
        self.pair_buf, self.sum_buf, self.chip_buf, self.sems = pair_buf, sum_buf, chip_buf, sems
        self.partner = plane.device(plane.chip, 1 - plane.core)

    def pair(self, r):
        source = self.part.at[r, :, 1 - self.plane.core]
        return remote(source, self.pair_buf.at[r], self.sems[0].at[r], self.sems[1].at[r], self.partner)

    def give(self, r, c):
        chip = self.plane.chip
        device = self.plane.device(c, self.plane.core)
        return remote(
            self.sum_buf.at[r, c], self.chip_buf.at[r, chip], self.sems[2].at[r, c], self.sems[3].at[r, chip], device
        )

    def take(self, r, c):
        device = self.plane.device(c, self.plane.core)
        return remote(self.sum_buf.at[r, c], self.chip_buf.at[r, c], self.sems[2].at[r, c], self.sems[3].at[r, c], device)

    def show(self, r, c, owner):
        block = self.out.at[r, owner, self.plane.core]
        device = self.plane.device(c, self.plane.core)
        return remote(block, block, self.sems[4].at[r, c], self.sems[5].at[r, owner], device)

    def hand(self, r, c, core):
        block = self.out.at[r, c, core]
        return remote(block, block, self.sems[6].at[r, c], self.sems[7].at[r, c], self.partner)

    def begin(self, r):
        self.pair(r).start()

    def settle(self, r):
        plane = self.plane
        self.pair(r).wait_recv()
        for c in plane.order[1:]:
            self.sum_buf[r, c] = self.part[r, c, plane.core] + self.pair_buf[r, c]
            self.give(r, c).start()

    def finalize(self, r):
        plane = self.plane
        chip, core, others = plane.chip, plane.core, plane.order[1:]
        total = self.part[r, chip, core] + self.pair_buf[r, chip]
        for c in others:
            self.take(r, c).wait_recv()
            total = total + self.chip_buf[r, c]
        self.out[r, chip, core] = total
        for c in others:
            self.show(r, c, chip).start()
        self.hand(r, chip, core).start()

    def forward(self, r):
        for c in self.plane.order[1:]:
            self.show(r, c, c).wait_recv()
            self.hand(r, c, self.plane.core).start()

    def arrive(self, r):
        for c in self.plane.order:
            self.hand(r, c, 1 - self.plane.core).wait_recv()

    def drain(self, stages):
        for r in stages:
            self.pair(r).wait_send()
            for c in self.plane.order[1:]:
                self.give(r, c).wait_send()
                self.show(r, c, self.plane.chip).wait_send()
            for c in self.plane.order:
                self.hand(r, c, self.plane.core).wait_send()


def eliminate(leaves):
    groups = NB // SUB
    index = lax.broadcasted_iota(jnp.int32, (SUB, 2 * NB), 0)
    wide = (SUB, 2 * NB)
    leaves = [list(rows) for rows in leaves]
    for panel in range(groups):
        first = panel * SUB
        columns = [
            {
                q: [jnp.broadcast_to(rows[q][:, first + k : first + k + 1], wide) for k in range(SUB)]
                for q in range(panel, groups)
            }
            for rows in leaves
        ]
        for k in range(SUB):
            for rows, cols in zip(leaves, columns):
                own = cols[panel]
                scale = lax.rsqrt(jnp.broadcast_to(own[k][k : k + 1], wide))
                pivot = jnp.broadcast_to(rows[panel][k : k + 1], wide) * scale
                weight = {q: cols[q][k] * scale for q in range(panel, groups)}
                across = weight[panel]
                below = jnp.where(index > k, across, 0.0)
                rows[panel] = jnp.where(index == k, pivot, rows[panel] - below * pivot)
                for j in range(k + 1, SUB):
                    factor = jnp.broadcast_to(across[j : j + 1], wide)
                    for q in range(panel, groups):
                        cols[q][j] = cols[q][j] - (below if q == panel else weight[q]) * factor
                for q in range(panel + 1, groups):
                    rows[q] = rows[q] - weight[q] * pivot
    return leaves


def factor(bound, window, work, done_block):
    columns, window_rows = window.shape
    top = window_rows // 2 + window_rows // 16
    low = window_rows // 2 - window_rows // 16
    eye = jnp.where(
        lax.broadcasted_iota(jnp.int32, (columns, columns), 0)
        == lax.broadcasted_iota(jnp.int32, (columns, columns), 1),
        1.0,
        0.0,
    )
    lane = lax.broadcasted_iota(jnp.int32, (columns, window_rows), 1)
    head = jnp.where(lane < bound, window, 0.0)
    tail = window - head
    spans = ((head, 0, (top + 127) // 128 * 128), (tail, low // 128 * 128, window_rows))
    counts = (bound, window_rows - bound)
    for leaf, (masked, start, stop) in enumerate(spans):
        part = masked[:, start:stop]
        gram = mm3(part, part, NT)
        work[leaf, :, :columns] = gram / counts[leaf].astype(jnp.float32)
        work[leaf, :, columns:] = eye
    small_eye = eye[:NB, :NB]
    for block in range(columns // NB):
        begin, end = block * NB, (block + 1) * NB
        aug = []
        for leaf in range(2):
            diagonal = jnp.concatenate([work[leaf, begin:end, begin:end], small_eye], axis=1)
            aug.append([diagonal[q * SUB : (q + 1) * SUB] for q in range(NB // SUB)])
        done = eliminate(aug)
        for leaf in range(2):
            inverse = jnp.concatenate(done[leaf], axis=0)[:, NB:]
            rows = mm3(inverse, work[leaf, begin:end, :])
            work[leaf, begin:end, :] = rows
            done_block(leaf, block, begin, end, rows[:, :columns])
            if end < columns:
                work[leaf, end:, :] = work[leaf, end:, :] - mm3(rows[:, end:columns], rows, TN)


def whole_kernel(
    bound_ref, pattern_ref, omega_ref, contrib_ref, assembled_ref, maps_ref, bases_ref, coupling_ref,
    gathered, contrib_buf, assembled_buf, pick, place, front, entries,
    part, window, pair_buf, sum_buf, chip_buf, work, upper, sibling, input_sems, *sems,
):
    plane = Plane()
    window_rows = assembled_buf.shape[1]
    columns, width = upper.shape[1], bases_ref.shape[0]
    held = (pick, place, front, entries)
    load_front = pltpu.make_async_copy(contrib_ref.at[0], contrib_buf, input_sems.at[0])
    load_entries = pltpu.make_async_copy(assembled_ref.at[0], assembled_buf, input_sems.at[1])
    load_front.start()
    load_entries.start()
    greet(plane)

    def prepare():
        load_front.wait()
        load_entries.wait()
        prepare_sketch(pattern_ref, contrib_buf, assembled_buf, maps_ref, held)

    stages = part.shape[0]
    row_count, row_pos = lax.axis_size("row"), lax.axis_index("row")
    summing = Reduce(plane, part, window, pair_buf, sum_buf, chip_buf, sems[6:14])
    if stages == row_count:

        def stage(block):
            sketch(gathered[block].reshape(columns // stages, window_rows), held, part.at[block])
            summing.begin(block)

        drain_gather, nearest = gather(
            omega_ref, gathered, sems[:6], prepare, stage, summing.settle, lambda block: None
        )
        nearest(summing.finalize)
        nearest(summing.forward)
        order = [lax.rem(row_pos + step, row_count) for step in range(row_count)]
    else:
        idle = lambda block: None
        drain_gather, nearest = gather(omega_ref, gathered, sems[:6], prepare, idle, idle, idle)
        sketch(gathered[...].reshape(columns, window_rows), held, part.at[0])
        summing.begin(0)
        summing.settle(0)
        summing.finalize(0)
        summing.forward(0)
        order = [0]
    for r in order:
        summing.arrive(r)
    drain_gather()
    summing.drain(order)

    near_send, near_recv = sems[14:]
    near = {"row": row_pos + 1 - 2 * (row_pos % 2)}

    def send(leaf, block):
        start = block * NB // 128 * 128
        rows = slice(block * NB, (block + 1) * NB)
        source, target = upper.at[leaf, rows, start:], sibling.at[leaf, rows, start:]
        return remote(source, target, near_send.at[leaf, block], near_recv.at[leaf, block], near)

    def done_block(leaf, block, begin, end, rows):
        keep = lax.broadcasted_iota(jnp.int32, rows.shape, 1) >= begin + lax.broadcasted_iota(
            jnp.int32, rows.shape, 0
        )
        upper[leaf, begin:end, :] = jnp.where(keep, rows, 0.0)
        send(leaf, block).start()

    bound = bound_ref[0]
    samples = window[...].reshape(columns, window_rows)
    factor(bound, samples, work, done_block)
    mine = pl.ds(pl.multiple_of(plane.group * width, width), width)
    inverse = jnp.concatenate([work[0, mine, columns:], work[1, mine, columns:]], axis=0)
    both = mm3(inverse, samples)
    lane = lax.broadcasted_iota(jnp.int32, (width, window_rows), 1)
    bases_ref[...] = jnp.where(lane < bound, both[:width], both[width:])
    for leaf in range(2):
        own = upper[leaf, mine, :]
        pieces = []
        for block in range(columns // NB):
            start = block * NB // 128 * 128
            send(leaf, block).wait_recv()
            pieces.append(mm3(own[:, start:], sibling[leaf, block * NB : (block + 1) * NB, start:], NT))
        coupling_ref[0, leaf] = jnp.concatenate(pieces, axis=1)
    for leaf in range(2):
        for block in range(columns // NB):
            send(leaf, block).wait_send()


def deliver_kernel(bases_ref, coupling_ref, bases_out, coupling_out):
    bases_out[...] = bases_ref[...]
    coupling_out[...] = coupling_ref[...]


def local(contrib, assembled, pattern, omega, row_maps, leaf_bounds):
    tile_rows, tile_cols = contrib.shape[1:]
    window_rows, own_width = omega.shape
    rows = lax.axis_size("row")
    chips = lax.axis_size("col") * lax.axis_size("child") // 2
    columns = own_width * rows
    width = columns // (2 * chips)
    own = omega.T.reshape(2, own_width // 2, window_rows)
    f32, bf16, dma = jnp.float32, jnp.bfloat16, pltpu.SemaphoreType.DMA
    any_space = pl.BlockSpec(memory_space=pl.ANY)
    stages = rows if columns // (rows * 2 * chips) >= SUB else 1
    piece = width // stages
    block = pltpu.VMEM((stages, chips, piece, window_rows), f32)
    split_window = pltpu.VMEM((stages, chips, 2, piece, window_rows), f32)
    bases, coupling = pl.pallas_call(
        whole_kernel,
        out_shape=(
            jax.ShapeDtypeStruct((width, window_rows), f32),
            jax.ShapeDtypeStruct((1, 2, width, columns), f32),
        ),
        in_specs=[SMEM, SMEM, VMEM, any_space, any_space, VMEM],
        out_specs=(VMEM, VMEM),
        scratch_shapes=[
            pltpu.VMEM((rows, 2, own_width // 2, window_rows), f32),
            pltpu.VMEM((tile_rows, tile_cols), f32),
            pltpu.VMEM((tile_rows, window_rows), f32),
            pltpu.VMEM((window_rows, tile_cols), bf16),
            pltpu.VMEM((window_rows, tile_rows), bf16),
            pltpu.VMEM((2, tile_rows, tile_cols), bf16),
            pltpu.VMEM((2, tile_rows, window_rows), bf16),
            split_window,
            split_window,
            block,
            block,
            block,
            pltpu.VMEM((2, columns, 2 * columns), f32),
            pltpu.VMEM((2, columns, columns), f32),
            pltpu.VMEM((2, columns, columns), f32),
            dma((2,)),
        ]
        + [dma((rows,))] * 5
        + [dma]
        + [dma((stages,))] * 2
        + [dma((stages, chips))] * 6
        + [dma((2, columns // NB))] * 2,
        compiler_params=pltpu.CompilerParams(
            collective_id=0, has_side_effects=True, vmem_limit_bytes=56 << 20
        ),
        name="front_samples",
    )(leaf_bounds, pattern, own, contrib, assembled, row_maps)
    bases, coupling = pl.pallas_call(
        deliver_kernel,
        out_shape=(
            jax.ShapeDtypeStruct(bases.shape, f32),
            jax.ShapeDtypeStruct(coupling.shape, f32),
        ),
        in_specs=[VMEM, VMEM],
        out_specs=(VMEM, VMEM),
        name="deliver",
    )(bases, coupling)
    return (bases.T, coupling)


def solution(mesh):
    in_specs = (
        P("child", "row", "col"),
        P("child", "row", "col"),
        P("row", "col"),
        P("col", "row"),
        P("child", None),
        P("row"),
    )
    out_specs = (P("row", ("child", "col")), P("row", None, ("child", "col"), None))
    return jax.shard_map(local, mesh=mesh, in_specs=in_specs, out_specs=out_specs, check_vma=False)
```
